128 devices in a mesh: row: 32 (over y, x, core), col: 4 (over z).
Axes of the slice: x: 4, y: 4, z: 4, core: 2. Of those that a mesh axis runs over, the one named last changes fastest.
Arguments:
- inverse_blocks: bfloat16 [32, 384, 256, 256], P('row', 'col'), may hold values from -6 to 6
- inverse_rows: int32 [32, 384], P('row', 'col'), may hold values from 0 to 95, as said below
- inverse_cols: int32 [32, 384], P('row', 'col'), may hold values from 0 to 95, as said below
- inverse_count: int32 [32, 4], P('row', 'col'), may hold values from 1 to 96, as said below
- panel_rows: int32 [64], replicated, may hold values from -1 to 95, as said below
- lower_old: bfloat16 [3, 64, 256, 256], P(None, 'row'), may hold values from -0.038085938 to 0.038085938
- lower_new: bfloat16 [3, 3, 256, 256], replicated, may hold values from -0.375 to 0.375
- diag_inverse: float32 [3, 256, 256], replicated, may hold values from -6 to 6
Outputs:
- panel_inverse: bfloat16 [3, 64, 256, 256], P(None, 'row', 'col')
- supernode_inverse: float32 [3, 3, 256, 256], replicated
The draws below stay inside these ranges and needn't reach their ends.
Inputs may be any that keep to these rules, and one draw needn't show every extreme that they name: `panel_rows`: for each row index r in order, 2 entries: distinct block rows congruent to r modulo the number of row indices, at least one, then -1 in the empty slots; some row index fills all 2 in every draw. `inverse_rows`: on row index r every slot names one of the panel rows of r, padding slots too. `inverse_cols`: on column index c every slot names a block column congruent to c modulo the number of column indices; positions may repeat, and repeated blocks add. `inverse_count`: slots 0 to count - 1 of a device's lists are live, the rest padding; one device reaches 96 in every draw.
All inputs are finite; a program needn't handle non-finite values.
Results may differ from the reference program's by a relative error of at most 0.0045.
Values may be sent and summed in bfloat16 or wider, within the bound.
A program may use at most 128 MiB of HBM per device.

```python
import jax
import jax.numpy as jnp
from jax import lax

B = 256
OLDB = 96
NSUP = 3
SLOTS = 2
KMAX = 96
ROW_GROUPS = 32
COL_GROUPS = 4
STORED = 384
ROWSLOTS = 64
N_COL = 4


def panel_pattern(key):
    base_key = jax.random.fold_in(key, 11)
    first_key, second_key, third_key = jax.random.split(base_key, 3)
    options = (OLDB + ROW_GROUPS - 1) // ROW_GROUPS
    device = jnp.arange(ROW_GROUPS, dtype=jnp.int32)[:, None]
    candidate = jnp.arange(options, dtype=jnp.int32)[None, :]
    scores = jax.random.randint(first_key, (ROW_GROUPS, options), 0, 1 << 20) * options + candidate
    usable = device + ROW_GROUPS * candidate < OLDB
    scores = jnp.where(usable, scores, (1 << 20) * options + candidate)
    ranking = jnp.argsort(scores, axis=1, stable=True)[:, :SLOTS].astype(jnp.int32)
    picked_rows = device + ROW_GROUPS * ranking
    counts = jax.random.randint(second_key, (ROW_GROUPS,), 1, SLOTS + 1)
    fullest = jax.random.randint(third_key, (), 0, ROW_GROUPS)
    counts = jnp.where(jnp.arange(ROW_GROUPS) == fullest, SLOTS, counts)
    pattern_rows = jnp.where(jnp.arange(SLOTS)[None, :] < counts[:, None], picked_rows, -1)
    return (pattern_rows.astype(jnp.int32), counts.astype(jnp.int32))


def draw_panel_rows(key, part):
    pattern_rows, counts = panel_pattern(key)
    return pattern_rows.reshape(-1)


def draw_inverse_rows(key, part):
    pattern_rows, counts = panel_pattern(key)
    picks = jax.random.randint(jax.random.fold_in(key, 23), (ROW_GROUPS, STORED), 0, 1 << 20) % counts[:, None]
    return jnp.take_along_axis(pattern_rows, picks, axis=1).astype(jnp.int32)


def draw_inverse_cols(key, part):
    column = jnp.arange(COL_GROUPS, dtype=jnp.int32)[None, :, None]
    options = (OLDB - column + COL_GROUPS - 1) // COL_GROUPS
    drawn = jax.random.randint(jax.random.fold_in(key, 29), (ROW_GROUPS, COL_GROUPS, KMAX), 0, 1 << 20) % options
    return (column + COL_GROUPS * drawn).reshape(ROW_GROUPS, STORED).astype(jnp.int32)


def draw_inverse_count(key, part):
    first_key, second_key, third_key = jax.random.split(jax.random.fold_in(key, 31), 3)
    first_draw = jax.random.randint(first_key, (ROW_GROUPS * COL_GROUPS,), 1, KMAX + 1)
    second_draw = jax.random.randint(second_key, (ROW_GROUPS * COL_GROUPS,), 1, KMAX + 1)
    counts = jnp.minimum(first_draw, second_draw)
    fullest = jax.random.randint(third_key, (), 0, ROW_GROUPS * COL_GROUPS)
    counts = jnp.where(jnp.arange(ROW_GROUPS * COL_GROUPS) == fullest, KMAX, counts)
    return counts.reshape(ROW_GROUPS, COL_GROUPS).astype(jnp.int32)


def level_of(key, extent, shards, least, high):
    def one(dim, shards_of):
        heights = jax.random.uniform(jax.random.fold_in(jax.random.fold_in(key, 6), dim), (shards_of,), jnp.float32, least / len(shards), high / len(shards))
        return jnp.repeat(jnp.exp(heights), extent[dim] // shards_of).reshape((-1,) + (1,) * (len(extent) - dim - 1))

    factor_of = one(*shards[0])
    for cut in shards[1:]:
        factor_of = factor_of * one(*cut)
    return factor_of


def normal_values(key, extent, width, bound, pieces=(), kind=jnp.bfloat16):
    values = width * jax.random.normal(key, extent, jnp.float32)
    if pieces:
        values = values * level_of(key, extent, pieces, -0.22, 0.18)
    return jnp.clip(values, -bound, bound).astype(kind)


def setup_inputs(seed: int = 0) -> dict:
    key_list = jax.random.split(jax.random.key(seed), 9)
    inverse_blocks = normal_values(key_list[0], (ROW_GROUPS, STORED, B, B), 1.0, 6.0, ((0, 32), (1, 4)))
    inverse_rows = draw_inverse_rows(jax.random.fold_in(key_list[8], 71), 0)
    inverse_cols = draw_inverse_cols(jax.random.fold_in(key_list[8], 71), 0)
    inverse_count = draw_inverse_count(jax.random.fold_in(key_list[8], 71), 0)
    panel_rows = draw_panel_rows(jax.random.fold_in(key_list[8], 71), 0)
    lower_old = normal_values(key_list[5], (NSUP, ROWSLOTS, B, B), (1.0 / (B * KMAX) ** 0.5), 0.038085938, ((1, 32),))
    lower_new = normal_values(key_list[6], (NSUP, NSUP, B, B), B ** -0.5, 0.375)
    diag_inverse = normal_values(key_list[7], (NSUP, B, B), 1.0, 6.0, (), jnp.float32)
    return dict(inverse_blocks=inverse_blocks, inverse_rows=inverse_rows, inverse_cols=inverse_cols, inverse_count=inverse_count, panel_rows=panel_rows, lower_old=lower_old, lower_new=lower_new, diag_inverse=diag_inverse)


exact_mode = lax.Precision.HIGHEST


def linked(blocks_new, left_node, right_node):
    if left_node == right_node:
        return blocks_new[(left_node, left_node)]
    if right_node > left_node:
        return blocks_new[(right_node, left_node)]
    return blocks_new[(left_node, right_node)].T


def reference(inverse_blocks, inverse_rows, inverse_cols, inverse_count, panel_rows, lower_old, lower_new, diag_inverse):
    block_width = inverse_blocks.shape[-1]
    supernodes = lower_old.shape[0]
    live_panel = panel_rows >= 0
    placement = jnp.where(live_panel, panel_rows, OLDB).astype(jnp.int32)
    member = jnp.zeros((OLDB + 1,), jnp.float32).at[placement].max(live_panel.astype(jnp.float32))
    masked = lower_old.astype(jnp.float32) * live_panel.astype(jnp.float32)[None, :, None, None]
    lower_dense = jnp.zeros((supernodes, OLDB + 1, block_width, block_width), jnp.float32).at[:, placement].add(masked)
    entries = inverse_rows.size
    slot_index = jnp.arange(entries, dtype=jnp.int32)
    flat_rows = inverse_rows.reshape(-1).astype(jnp.int32)
    flat_cols = inverse_cols.reshape(-1).astype(jnp.int32)
    device_row = slot_index // (N_COL * KMAX)
    device_col = (slot_index // KMAX) % N_COL
    within = slot_index % KMAX
    is_live = within < inverse_count[device_row, device_col]
    useful = is_live & (member[flat_rows] > 0) & (member[flat_cols] > 0)
    ordering = jnp.argsort(jnp.where(useful, 0, 1).astype(jnp.int32), stable=True).astype(jnp.int32)
    used_count = jnp.sum(useful.astype(jnp.int32))
    flat_blocks = inverse_blocks.reshape(entries, block_width, block_width)

    def accumulate(group_index, running):
        selected = lax.dynamic_slice_in_dim(ordering, group_index * 8, 8)
        is_valid = (group_index * 8 + jnp.arange(8, dtype=jnp.int32)) < used_count
        chosen = flat_blocks[selected].astype(jnp.float32)
        factors = lower_dense[:, flat_cols[selected]]
        products = jnp.einsum("kab,skbc->skac", chosen, factors, precision=exact_mode)
        products = products * is_valid.astype(jnp.float32)[None, :, None, None]
        return running.at[:, flat_rows[selected]].add(products)

    partial_value = lax.fori_loop(0, (used_count + 7) // 8, accumulate,
                            jnp.zeros((supernodes, OLDB + 1, block_width, block_width), jnp.float32))
    lower_links = lower_new.astype(jnp.float32)
    panels = []
    blocks_new = {}
    for node in range(supernodes):
        running = partial_value[node]
        for earlier in range(node):
            running = running + jnp.einsum("nab,bc->nac", panels[earlier].astype(jnp.float32), lower_links[node, earlier], precision=exact_mode)
        current = (-running * member[:, None, None]).astype(jnp.bfloat16)
        current_wide = current.astype(jnp.float32)
        for earlier in range(node):
            crossed = jnp.einsum("nab,nac->bc", panels[earlier].astype(jnp.float32), lower_dense[node], precision=exact_mode)
            for another in range(node):
                crossed = crossed + jnp.dot(linked(blocks_new, earlier, another), lower_links[node, another], precision=exact_mode)
            blocks_new[(node, earlier)] = -crossed
        diagonal_block = diag_inverse[node] - jnp.einsum("nab,nac->bc", lower_dense[node], current_wide, precision=exact_mode)
        for earlier in range(node):
            diagonal_block = diagonal_block - jnp.dot(lower_links[node, earlier].T, blocks_new[(node, earlier)], precision=exact_mode)
        blocks_new[(node, node)] = diagonal_block
        panels.append(current)
    panel_inverse = jnp.stack([panel[placement] for panel in panels])
    empty_block = jnp.zeros((block_width, block_width), jnp.float32)
    supernode_inverse = jnp.stack([
        jnp.stack([blocks_new[(node, earlier)] if earlier <= node else empty_block for earlier in range(supernodes)])
        for node in range(supernodes)])
    return panel_inverse, supernode_inverse
```

```python
import functools

import jax
import jax.numpy as jnp
from jax import lax
from jax.experimental import pallas as pl
from jax.experimental.pallas import tpu as pltpu
from jax.sharding import PartitionSpec as P

MESH = pl.DeviceIdType.MESH
GROUP = 4
BUNDLES = (3, 2, 1)
F32 = jnp.float32
BF16 = jnp.bfloat16


def slot_lists(rows, cols, count, own_rows, cand_rows):
    kmax = rows.shape[0]
    groups = kmax // GROUP + 1
    slots = jnp.arange(kmax, dtype=jnp.int32)
    matches = cols[:, None] == cand_rows[None, :]
    useful = jnp.any(matches, axis=1) & (slots < count)
    position = jnp.sum(
        jnp.where(matches, jnp.arange(cand_rows.shape[0], dtype=jnp.int32)[None, :], 0), axis=1
    )
    mine = useful[None, :] & (rows[None, :] == own_rows[:, None])
    before = slots[None, :] < slots[:, None]
    rank = jnp.sum((before[None] & mine[:, None, :]).astype(jnp.int32), axis=2)
    first = jnp.sum(mine[0].astype(jnp.int32))
    start = (first + GROUP - 1) // GROUP * GROUP
    place = jnp.where(mine[0], rank[0], jnp.where(mine[1], start + rank[1], -1))
    hit = place[None, :] == jnp.arange(groups * GROUP, dtype=jnp.int32)[:, None]
    slot_at = jnp.where(jnp.any(hit, axis=1), jnp.sum(jnp.where(hit, slots[None, :], 0), axis=1), kmax)
    cand_at = jnp.sum(jnp.where(hit, position[None, :], 0), axis=1)
    is_first = (jnp.arange(groups, dtype=jnp.int32) * GROUP < start).astype(F32)
    return slot_at, cand_at, is_first


def kernel(
    slot_at, cand_at, is_first, low, blocks_hbm, new_hbm, diag_hbm,
    panel_out, super_out,
    blocks, lo0, lo1, lo2, acc0, acc1, acc2, new, diag,
    rs_a, rs_b, rs_p, rs_m, u_all,
    g0, g1, g2, c0, c1, c2, h0, h1, h2, zr0, zr1, zr2, hz0, hz1, hz2,
    xr0, xr1, xr2, hx0, hx1, hx2, yr0, yr1, yr2, f0, f1, f2,
    local_sem, lo_send, lo_recv, rs_send, rs_recv, ar_send, ar_recv,
):
    lo = (lo0, lo1, lo2)
    acc = (acc0, acc1, acc2)
    row = lax.axis_index("row")
    z = lax.axis_index("col")
    y = row // 8
    x = (row // 2) % 4
    k = row % 2
    sib = (y * 8 + x * 2 + (1 - k), z)

    def at(dx=0, dy=0, dz=0):
        return ((y + dy + 4) % 4 * 8 + (x + dx + 4) % 4 * 2 + k, (z + dz + 4) % 4)

    barrier = pltpu.get_barrier_semaphore()
    partners = [sib]
    for d in (1, 2, 3):
        partners += [at(dx=d), at(dy=d), at(dz=d)]
    for dev in partners:
        pl.semaphore_signal(barrier, inc=1, device_id=dev, device_id_type=MESH)

    block_copy = pltpu.make_async_copy(blocks_hbm.at[0], blocks.at[pl.ds(0, 96)], local_sem.at[0])
    new_copy = pltpu.make_async_copy(new_hbm, new, local_sem.at[1])
    diag_copy = pltpu.make_async_copy(diag_hbm, diag, local_sem.at[2])
    block_copy.start()
    new_copy.start()
    diag_copy.start()
    blocks[96] = jnp.zeros((256, 256), BF16)

    src_x = z // 2
    src_k = z % 2
    is_src = x % 2 == src_x
    def piece(half, yy, slot):
        return ((yy + 8) % 4 * 2 + half) * 2 + slot

    own_half = x // 2
    left_half = (x + 3) % 4 // 2
    right_half = (x + 1) % 4 // 2
    far_half = 1 - own_half

    sent = {"src": [], "mid": []}

    def send(role, t, cand, dev):
        n = len([1 for (tt, _) in sent[role] if tt == t])
        sent[role].append((t, n))
        pltpu.make_async_remote_copy(
            lo[t].at[cand], lo[t].at[cand], lo_send.at[t, n], lo_recv.at[t, cand],
            device_id=dev, device_id_type=MESH,
        ).start()

    def arrived(t, cand):
        pltpu.make_async_remote_copy(
            lo[t].at[cand], lo[t].at[cand], lo_send.at[t, 0], lo_recv.at[t, cand],
            device_id=sib, device_id_type=MESH,
        ).wait_recv()

    turn = 1 - 2 * k

    def src_step(t, step):
        wide = t == 1
        if step == 1:
            own = piece(own_half, y, k)
            for dev in (at(dx=1), at(dx=-1), at(dy=1), at(dy=-1)):
                send("src", t, own, dev)
        if step == 2:
            c = piece(own_half, y - turn, k)
            arrived(t, c)
            send("src", t, c, at(dy=turn))
            if wide:
                send("src", t, c, at(dx=1))
                send("src", t, c, at(dx=-1))
            send("src", t, c, sib)
            c = piece(own_half, y + turn, k)
            arrived(t, c)
            if wide:
                send("src", t, c, at(dx=1))
                send("src", t, c, at(dx=-1))
            send("src", t, c, sib)
            c = piece(far_half, y, k)
            arrived(t, c)
            send("src", t, c, sib)
        if step == 3:
            c = piece(own_half, y + 2, k)
            arrived(t, c)
            if wide:
                send("src", t, c, at(dx=1))
                send("src", t, c, at(dx=-1))
            send("src", t, c, sib)
            for d in (1, 3):
                c = piece(far_half, y + d, k)
                arrived(t, c)
                send("src", t, c, sib)
        if step == 4:
            c = piece(far_half, y + 2, k)
            arrived(t, c)
            send("src", t, c, sib)

    def mid_step(t, step):
        wide = t == 1
        for d in {1: (0,), 2: (3, 1), 3: (2,), 4: ()}[step]:
            c = piece(left_half, y + d, k)
            arrived(t, c)
            if not wide and d == 0:
                send("mid", t, c, at(dy=1))
                send("mid", t, c, at(dy=-1))
            if not wide and d == 3:
                send("mid", t, c, at(dy=1))
            if d in (0, 1):
                send("mid", t, c, at(dx=1))
            send("mid", t, c, sib)
            c = piece(right_half, y + d, k)
            arrived(t, c)
            if not wide and d == 0:
                send("mid", t, c, at(dy=1))
                send("mid", t, c, at(dy=-1))
            if not wide and d == 1:
                send("mid", t, c, at(dy=-1))
            if d in (2, 3):
                send("mid", t, c, at(dx=-1))
            send("mid", t, c, sib)

    def gather_steps(*steps):
        @pl.when(is_src)
        def _():
            for t, step in steps:
                src_step(t, step)

        @pl.when(jnp.logical_not(is_src))
        def _():
            for t, step in steps:
                mid_step(t, step)

    def from_sibling(t):
        @pl.when(is_src)
        def _():
            for d in (1, 2, 3):
                arrived(t, piece(own_half, y + d, 1 - k))
            for d in range(4):
                arrived(t, piece(far_half, y + d, 1 - k))

        @pl.when(jnp.logical_not(is_src))
        def _():
            for d in range(4):
                arrived(t, piece(left_half, y + d, 1 - k))
                arrived(t, piece(right_half, y + d, 1 - k))

    def multiply(t):
        acc[t][...] = jnp.zeros((2, 256, 256), F32)

        def body(g, carry):
            left = [blocks[slot_at[g * GROUP + i]] for i in range(GROUP)]
            right = [lo[t][cand_at[g * GROUP + i]] for i in range(GROUP)]
            product = jnp.dot(
                jnp.concatenate(left, axis=1), jnp.concatenate(right, axis=0), preferred_element_type=F32
            )
            weight = is_first[g]
            acc[t][0] += product * weight
            acc[t][1] += product * (1.0 - weight)
            return carry

        lax.fori_loop(0, 96 // GROUP + 1, body, 0)

    def quarter(d):
        return pl.ds(pl.multiple_of((z + d) % 4 * 64, 64), 64)

    def rs_copy(t, n):
        a = acc[t]
        src, dst, dev = (
            (a.at[0, quarter(2)], rs_a.at[t], at(dz=1)),
            (a.at[1, quarter(2)], rs_b.at[t], at(dz=3)),
            (a.at[1, quarter(1)], rs_p.at[t, 1], at(dz=1)),
            (a.at[0, quarter(3)], rs_m.at[t, 0], at(dz=3)),
            (a.at[0, quarter(1)], rs_p.at[t, 0], at(dz=1)),
            (a.at[1, quarter(3)], rs_m.at[t, 1], at(dz=3)),
        )[n]
        return pltpu.make_async_remote_copy(
            src, dst, rs_send.at[t, n], rs_recv.at[t, n], device_id=dev, device_id_type=MESH
        )

    def rs_first(t):
        for n in range(4):
            rs_copy(t, n).start()

    def rs_second(t):
        rs_copy(t, 0).wait_recv()
        acc[t][0, quarter(1)] += rs_a[t]
        rs_copy(t, 4).start()
        rs_copy(t, 1).wait_recv()
        acc[t][1, quarter(3)] += rs_b[t]
        rs_copy(t, 5).start()

    def rs_third(t):
        for n in (2, 3, 4, 5):
            rs_copy(t, n).wait_recv()
        return (acc[t][:, quarter(0)] + (rs_p[t] + rs_m[t])).reshape(128, 256)

    def low_rows(t):
        return low[t, :, pl.ds(pl.multiple_of(z * 64, 64), 64), :].reshape(128, 256)

    def across(left, right):
        return lax.dot_general(left, right, (((0,), (0,)), ((), ())), preferred_element_type=F32)

    g = (g0, g1, g2)

    def panel(t):
        running = rs_third(t)
        for e in range(t):
            running = running + jnp.dot(u_all[e], new[t, e], preferred_element_type=F32)
        current = (-running).astype(BF16)
        u_all[t] = current
        panel_out[t] = current.reshape(2, 64, 256)
        if t == 0:
            g0[0] = across(current, low_rows(1))
            g0[1] = across(current, low_rows(2))
            g0[2] = across(low_rows(0), current)
        elif t == 1:
            g1[0] = across(current, low_rows(2))
            g1[1] = across(low_rows(1), current)
        else:
            g2[0] = across(low_rows(2), current)

    def ar(b, phase):
        nb = BUNDLES[b]
        gb, cb, hb, zb, hzb, xb, hxb, yb, fb = (
            (g0, c0, h0, zr0, hz0, xr0, hx0, yr0, f0),
            (g1, c1, h1, zr1, hz1, xr1, hx1, yr1, f1),
            (g2, c2, h2, zr2, hz2, xr2, hx2, yr2, f2),
        )[b]

        def ds(start, size):
            return pl.ds(pl.multiple_of(start, size), size)

        def copy(n, src, dst, dev):
            return pltpu.make_async_remote_copy(
                src, dst, ar_send.at[b, n], ar_recv.at[b, n], device_id=dev, device_id_type=MESH
            )

        def core():
            return [copy(0, gb.at[:, ds(128 * (1 - k), 128)], cb, sib)]

        def over_z():
            return [
                copy(d, hb.at[:, ds((z + d) % 4 * 32, 32)], zb.at[d - 1], at(dz=d)) for d in (1, 2, 3)
            ]

        def over_x():
            return [
                copy(3 + d, hzb.at[:, ds((x + d) % 4 * 8, 8)], xb.at[d - 1], at(dx=d)) for d in (1, 2, 3)
            ]

        def over_y():
            return [copy(6 + d, hxb, yb.at[y], at(dy=d)) for d in (1, 2, 3)]

        base = 128 * k + 32 * z + 8 * x

        def back_x():
            part = fb.at[:, ds(base, 8)]
            return [copy(9 + d, part, part, at(dx=d)) for d in (1, 2, 3)]

        def back_z():
            part = fb.at[:, ds(128 * k + 32 * z, 32)]
            return [copy(12 + d, part, part, at(dz=d)) for d in (1, 2, 3)]

        def back_core():
            part = fb.at[:, ds(128 * k, 128)]
            return [copy(16, part, part, sib)]

        stages = (core, over_z, over_x, over_y, back_x, back_z, back_core)
        if phase > 0:
            for c in stages[phase - 1]():
                c.wait_recv()
        if phase == 1:
            hb[...] = gb[:, ds(128 * k, 128)] + cb[...]
        if phase == 2:
            hzb[...] = hb[:, ds(32 * z, 32)] + (zb[0] + zb[1] + zb[2])
        if phase == 3:
            hxb[...] = hzb[:, ds(8 * x, 8)] + (xb[0] + xb[1] + xb[2])
            yb[y] = hxb[...]
        if phase == 4:
            fb[:, ds(base, 8)] = (yb[0] + yb[1]) + (yb[2] + yb[3])
        if phase < 7:
            for c in stages[phase]():
                c.start()
        if phase == 7:
            for stage in stages:
                for c in stage():
                    c.wait_send()

    def times(value, factor, turned=False):
        high = value.astype(BF16)
        rest = value - high.astype(F32)
        middle = rest.astype(BF16)
        tail = (rest - middle.astype(F32)).astype(BF16)
        total = None
        for part in (tail, middle, high):
            if turned:
                term = across(factor, part)
            else:
                term = jnp.dot(part, factor, preferred_element_type=F32)
            total = term if total is None else total + term
        return total

    pl.semaphore_wait(barrier, len(partners))

    @pl.when(is_src & (k == src_k))
    def _():
        own = piece(own_half, y, 0)
        for t in range(3):
            for s in range(2):
                lo[t][own + s] = low[t, s]
                pltpu.make_async_remote_copy(
                    lo[t].at[own + s], lo[t].at[own + s], lo_send.at[t, 30 + s], lo_recv.at[t, own + s],
                    device_id=sib, device_id_type=MESH,
                ).start()

    @pl.when(is_src & (k != src_k))
    def _():
        own = piece(own_half, y, 0)
        for t in range(3):
            for s in range(2):
                arrived(t, own + s)

    gather_steps((0, 1), (1, 1))

    @pl.when(is_src)
    def _():
        src_step(2, 1)

    gather_steps((0, 2), (1, 2))

    @pl.when(jnp.logical_not(is_src))
    def _():
        mid_step(2, 1)

    gather_steps((0, 3), (1, 3), (0, 4))
    from_sibling(0)
    block_copy.wait()
    multiply(0)
    rs_first(0)
    gather_steps((2, 2), (1, 4))
    from_sibling(1)
    rs_second(0)
    multiply(1)
    rs_first(1)
    new_copy.wait()
    panel(0)
    ar(0, 0)
    gather_steps((2, 3))
    rs_second(1)
    ar(0, 1)
    gather_steps((2, 4))
    from_sibling(2)
    multiply(2)
    rs_first(2)
    panel(1)
    ar(1, 0)
    ar(0, 2)
    rs_second(2)
    ar(1, 1)
    ar(0, 3)
    panel(2)
    ar(2, 0)
    ar(1, 2)
    ar(0, 4)
    ar(2, 1)
    ar(1, 3)
    ar(0, 5)
    ar(2, 2)
    ar(1, 4)
    ar(0, 6)
    ar(2, 3)
    ar(1, 5)
    ar(0, 7)
    diag_copy.wait()
    y00 = diag[0] - f0[2]
    y10 = -(f0[0] + times(y00, new[1, 0]))
    super_out[0, 0] = y00
    super_out[1, 0] = y10
    ar(2, 4)
    ar(1, 6)
    nothing = jnp.zeros((256, 256), F32)
    super_out[0, 1] = nothing
    super_out[0, 2] = nothing
    super_out[1, 2] = nothing
    y20 = -(f0[1] + (times(y00, new[2, 0]) + times(y10, new[2, 1])))
    super_out[2, 0] = y20
    ar(2, 5)
    ar(1, 7)
    y11 = (diag[1] - f1[1]) - times(y10, new[1, 0], True)
    super_out[1, 1] = y11
    y21 = -(f1[0] + (times(y10.T, new[2, 0]) + times(y11, new[2, 1])))
    super_out[2, 1] = y21
    ar(2, 6)
    rest = diag[2] - (times(y20, new[2, 0], True) + times(y21, new[2, 1], True))
    ar(2, 7)
    super_out[2, 2] = rest - f2[0]

    for t in range(3):
        for n in range(6):
            rs_copy(t, n).wait_send()

    def send_done(t, n):
        pltpu.make_async_remote_copy(
            lo[t].at[0], lo[t].at[0], lo_send.at[t, n], lo_recv.at[t, 0],
            device_id=sib, device_id_type=MESH,
        ).wait_send()

    @pl.when(is_src & (k == src_k))
    def _():
        for t in range(3):
            for s in range(2):
                send_done(t, 30 + s)

    @pl.when(is_src)
    def _():
        for t, n in sent["src"]:
            send_done(t, n)

    @pl.when(jnp.logical_not(is_src))
    def _():
        for t, n in sent["mid"]:
            send_done(t, n)


def per_device(
    inverse_blocks,
    inverse_rows,
    inverse_cols,
    inverse_count,
    panel_rows,
    lower_old,
    lower_new,
    diag_inverse,
):
    row_me = lax.axis_index("row")
    col_me = lax.axis_index("col")
    own_rows = lax.dynamic_slice_in_dim(panel_rows, row_me * 2, 2)
    cand_rows = lax.dynamic_index_in_dim(panel_rows.reshape(8, 4, 2), col_me, 1, False).reshape(16)
    lists = slot_lists(inverse_rows[0], inverse_cols[0], inverse_count[0, 0], own_rows, cand_rows)
    smem = pl.BlockSpec(memory_space=pltpu.SMEM)
    vmem = pl.BlockSpec(memory_space=pltpu.VMEM)
    hbm = pl.BlockSpec(memory_space=pl.ANY)

    def each(*shape):
        return [pltpu.VMEM(tuple(nb if s is None else s for s in shape), F32) for nb in BUNDLES]

    return pl.pallas_call(
        kernel,
        out_shape=(
            jax.ShapeDtypeStruct((3, 2, 64, 256), BF16),
            jax.ShapeDtypeStruct((3, 3, 256, 256), F32),
        ),
        in_specs=[smem, smem, smem, vmem, hbm, hbm, hbm],
        out_specs=(vmem, vmem),
        scratch_shapes=[
            pltpu.VMEM((97, 256, 256), BF16),
            *[pltpu.VMEM((16, 256, 256), BF16)] * 3,
            *[pltpu.VMEM((2, 256, 256), F32)] * 3,
            pltpu.VMEM((3, 3, 256, 256), BF16),
            pltpu.VMEM((3, 256, 256), F32),
            pltpu.VMEM((3, 64, 256), F32),
            pltpu.VMEM((3, 64, 256), F32),
            pltpu.VMEM((3, 2, 64, 256), F32),
            pltpu.VMEM((3, 2, 64, 256), F32),
            pltpu.VMEM((3, 128, 256), BF16),
            *each(None, 256, 256),
            *each(None, 128, 256),
            *each(None, 128, 256),
            *each(3, None, 32, 256),
            *each(None, 32, 256),
            *each(3, None, 8, 256),
            *each(None, 8, 256),
            *each(4, None, 8, 256),
            *each(None, 256, 256),
            pltpu.SemaphoreType.DMA((3,)),
            pltpu.SemaphoreType.DMA((3, 32)),
            pltpu.SemaphoreType.DMA((3, 16)),
            pltpu.SemaphoreType.DMA((3, 6)),
            pltpu.SemaphoreType.DMA((3, 6)),
            pltpu.SemaphoreType.DMA((3, 17)),
            pltpu.SemaphoreType.DMA((3, 17)),
        ],
        compiler_params=pltpu.CompilerParams(
            collective_id=0, has_side_effects=True, vmem_limit_bytes=52 * 2**20
        ),
    )(*lists, lower_old, inverse_blocks, lower_new, diag_inverse)


def solution(mesh):
    placed = (
        P("row", "col", None, None),
        P("row", "col"),
        P("row", "col"),
        P("row", "col"),
        P(),
        P(None, "row", None, None),
        P(),
        P(),
    )
    return jax.shard_map(
        per_device,
        mesh=mesh,
        in_specs=placed,
        out_specs=(P(None, "row", "col", None), P()),
        check_vma=False,
    )
```

```python
import functools

import jax
import jax.numpy as jnp
from jax import lax
from jax.experimental import pallas as pl
from jax.experimental.pallas import tpu as pltpu
from jax.sharding import PartitionSpec as P

MESH = pl.DeviceIdType.MESH
GROUP = 4
BUNDLES = (3, 2, 1)
PLANE = tuple((dx, dy) for dy in (1, 3, 0, 2) for dx in (1, 3, 0, 2) if (dx, dy) != (0, 0))
F32 = jnp.float32
BF16 = jnp.bfloat16


def slot_lists(rows, cols, count, panel_rows, row, col):
    kmax = rows.shape[1]
    slot = lax.broadcasted_iota(jnp.int32, (kmax, kmax), 0)
    other = lax.broadcasted_iota(jnp.int32, (kmax, kmax), 1)

    def upright(line):
        return jnp.sum(jnp.where(slot == other, jnp.broadcast_to(line, (kmax, kmax)), 0), axis=1, keepdims=True)

    stored_row, stored_col = upright(rows), upright(cols)
    index = lax.broadcasted_iota(jnp.int32, (kmax, 1), 0)
    live = index < count
    useful = jnp.zeros((kmax, 1), jnp.int32)
    position = jnp.zeros((kmax, 1), jnp.int32)
    for i in range(8):
        for j in range(2):
            same = stored_col == panel_rows[(i * 4 + col) * 2 + j]
            useful = jnp.where(same & live, 1, useful)
            position = jnp.where(same, i * 2 + j, position)
    mine = [jnp.where(stored_row == panel_rows[row * 2 + p], useful, 0) for p in range(2)]
    flat = [jnp.sum(jnp.where(slot == other, jnp.broadcast_to(m, (kmax, kmax)), 0), axis=0, keepdims=True) for m in mine]
    rank = [
        jnp.sum(jnp.where(other < slot, jnp.broadcast_to(f, (kmax, kmax)), 0), axis=1, keepdims=True) for f in flat
    ]
    first = jnp.sum(jnp.broadcast_to(flat[0], (8, kmax)), axis=1, keepdims=True)[0:1]
    padding = jnp.where(first % GROUP == 0, 0, GROUP - first % GROUP)
    start = first + padding
    place = jnp.where(mine[0] == 1, rank[0], jnp.where(mine[1] == 1, start + rank[1], -1))
    hit = place == lax.broadcasted_iota(jnp.int32, (kmax, 128), 1)
    filled = jnp.sum(jnp.where(hit, 1, 0), axis=0, keepdims=True)
    slot_at = jnp.sum(jnp.where(hit, index, 0), axis=0, keepdims=True)
    cand_at = jnp.sum(jnp.where(hit, position, 0), axis=0, keepdims=True)
    lane = lax.broadcasted_iota(jnp.int32, (1, 128), 1)
    is_first = jnp.where(lane * GROUP < start, 1, 0)
    return jnp.where(filled == 1, slot_at, kmax), cand_at, is_first


def kernel(
    rows, cols, count, panel_rows, low, blocks_hbm, new_hbm, diag_hbm,
    panel_out, super_out,
    lists, table,
    blocks, lo0, lo1, lo2, acc0, acc1, acc2, new, diag,
    rs_a, rs_b, rs_p, rs_m, u_all,
    g0, g1, g2, c0, c1, c2, h0, h1, h2, p0, p1, p2, s0, s1, s2, y0, y1, y2, f0, f1, f2,
    local_sem, lo_send, lo_recv, rs_send, rs_recv, ar_send, ar_recv,
):
    lo = (lo0, lo1, lo2)
    acc = (acc0, acc1, acc2)
    row = lax.axis_index("row")
    z = lax.axis_index("col")
    y = row // 8
    x = (row // 2) % 4
    k = row % 2
    sib = (y * 8 + x * 2 + (1 - k), z)

    def at(dx=0, dy=0, dz=0):
        return ((y + dy + 4) % 4 * 8 + (x + dx + 4) % 4 * 2 + k, (z + dz + 4) % 4)

    barrier = pltpu.get_barrier_semaphore()
    partners = [sib]
    partners += [at(dx=dx, dy=dy) for dx, dy in PLANE]
    partners += [at(dz=d) for d in (1, 2, 3)]
    for dev in partners:
        pl.semaphore_signal(barrier, inc=1, device_id=dev, device_id_type=MESH)

    block_copy = pltpu.make_async_copy(blocks_hbm.at[0], blocks.at[pl.ds(0, 96)], local_sem.at[0])
    new_copy = pltpu.make_async_copy(new_hbm, new, local_sem.at[1])
    diag_copy = pltpu.make_async_copy(diag_hbm, diag, local_sem.at[2])
    block_copy.start()
    new_copy.start()
    diag_copy.start()
    blocks[96] = jnp.zeros((256, 256), BF16)

    src_x = z // 2
    src_k = z % 2
    is_src = x % 2 == src_x
    def piece(half, yy, slot):
        return ((yy + 8) % 4 * 2 + half) * 2 + slot

    own_half = x // 2
    left_half = (x + 3) % 4 // 2
    right_half = (x + 1) % 4 // 2
    far_half = 1 - own_half

    sent = {"src": [], "mid": []}

    def send(role, t, cand, dev):
        n = len([1 for (tt, _) in sent[role] if tt == t])
        sent[role].append((t, n))
        pltpu.make_async_remote_copy(
            lo[t].at[cand], lo[t].at[cand], lo_send.at[t, n], lo_recv.at[t, cand],
            device_id=dev, device_id_type=MESH,
        ).start()

    def arrived(t, cand):
        pltpu.make_async_remote_copy(
            lo[t].at[cand], lo[t].at[cand], lo_send.at[t, 0], lo_recv.at[t, cand],
            device_id=sib, device_id_type=MESH,
        ).wait_recv()

    def src_step(t, step):
        if step == 1:
            own = piece(own_half, y, k)
            for dev in (at(dx=1), at(dx=-1), at(dy=1), at(dy=-1), at(dy=2)):
                send("src", t, own, dev)
        if step == 2:
            for d in (1, 3):
                c = piece(own_half, y + d, k)
                arrived(t, c)
                send("src", t, c, sib)
        if step == 3:
            c = piece(own_half, y + 2, k)
            arrived(t, c)
            send("src", t, c, at(dx=1))
            send("src", t, c, at(dx=-1))
            send("src", t, c, sib)
        if step >= 4:
            for d in {4: (0,), 5: (1, 3), 6: (2,)}[step]:
                c = piece(far_half, y + d, k)
                arrived(t, c)
                send("src", t, c, sib)

    def mid_step(t, step):
        for d in {1: (0,), 2: (3, 1), 3: (2,)}[step]:
            c = piece(left_half, y + d, k)
            arrived(t, c)
            if d == 0:
                send("mid", t, c, at(dy=1))
                send("mid", t, c, at(dy=-1))
            if d in (0, 1):
                send("mid", t, c, at(dx=1))
            send("mid", t, c, sib)
            c = piece(right_half, y + d, k)
            arrived(t, c)
            if d == 0:
                send("mid", t, c, at(dy=1))
                send("mid", t, c, at(dy=-1))
            if d in (2, 3):
                send("mid", t, c, at(dx=-1))
            send("mid", t, c, sib)

    def gather_steps(src_steps, mid_steps):
        @pl.when(is_src)
        def _():
            for t, step in src_steps:
                src_step(t, step)

        @pl.when(jnp.logical_not(is_src))
        def _():
            for t, step in mid_steps:
                mid_step(t, step)

    def from_sibling(t):
        @pl.when(is_src)
        def _():
            for d in (1, 2, 3):
                arrived(t, piece(own_half, y + d, 1 - k))
            for d in range(4):
                arrived(t, piece(far_half, y + d, 1 - k))

        @pl.when(jnp.logical_not(is_src))
        def _():
            for d in range(4):
                arrived(t, piece(left_half, y + d, 1 - k))
                arrived(t, piece(right_half, y + d, 1 - k))

    def multiply(t, begin, end):
        if begin == 0:
            acc[t][...] = jnp.zeros((2, 256, 256), F32)

        def body(g, carry):
            left = [blocks[table[0, g * GROUP + i]] for i in range(GROUP)]
            right = [lo[t][table[1, g * GROUP + i]] for i in range(GROUP)]
            product = jnp.dot(
                jnp.concatenate(left, axis=1), jnp.concatenate(right, axis=0), preferred_element_type=F32
            )
            weight = table[2, g].astype(F32)
            acc[t][0] += product * weight
            acc[t][1] += product * (1.0 - weight)
            return carry

        lax.fori_loop(begin, end, body, 0, unroll=5)

    def quarter(d):
        return pl.ds(pl.multiple_of((z + d) % 4 * 64, 64), 64)

    def rs_copy(t, n):
        a = acc[t]
        src, dst, dev = (
            (a.at[0, quarter(2)], rs_a.at[t], at(dz=1)),
            (a.at[1, quarter(2)], rs_b.at[t], at(dz=3)),
            (a.at[1, quarter(1)], rs_p.at[t, 1], at(dz=1)),
            (a.at[0, quarter(3)], rs_m.at[t, 0], at(dz=3)),
            (a.at[0, quarter(1)], rs_p.at[t, 0], at(dz=1)),
            (a.at[1, quarter(3)], rs_m.at[t, 1], at(dz=3)),
        )[n]
        return pltpu.make_async_remote_copy(
            src, dst, rs_send.at[t, n], rs_recv.at[t, n], device_id=dev, device_id_type=MESH
        )

    def rs_first(t):
        for n in range(4):
            rs_copy(t, n).start()

    def rs_second(t):
        rs_copy(t, 0).wait_recv()
        acc[t][0, quarter(1)] += rs_a[t]
        rs_copy(t, 4).start()
        rs_copy(t, 1).wait_recv()
        acc[t][1, quarter(3)] += rs_b[t]
        rs_copy(t, 5).start()

    def rs_third(t):
        for n in (2, 3, 4, 5):
            rs_copy(t, n).wait_recv()
        return (acc[t][:, quarter(0)] + (rs_p[t] + rs_m[t])).reshape(128, 256)

    def low_rows(t):
        return low[t, :, pl.ds(pl.multiple_of(z * 64, 64), 64), :].reshape(128, 256)

    def across(left, right):
        return lax.dot_general(left, right, (((0,), (0,)), ((), ())), preferred_element_type=F32)

    g = (g0, g1, g2)

    def earlier(t):
        total = jnp.dot(u_all[0], new[t, 0], preferred_element_type=F32)
        for e in range(1, t):
            total = total + jnp.dot(u_all[e], new[t, e], preferred_element_type=F32)
        return total

    def panel(t):
        running = rs_third(t)
        if t > 0:
            running = running + earlier(t)
        current = (-running).astype(BF16)
        u_all[t] = current
        panel_out[t] = current.reshape(2, 64, 256)
        if t == 0:
            g0[0] = across(current, low_rows(1))
            g0[1] = across(current, low_rows(2))
            g0[2] = across(low_rows(0), current)
        elif t == 1:
            g1[0] = across(current, low_rows(2))
            g1[1] = across(low_rows(1), current)

    def halves(value):
        high = value.astype(BF16)
        return high, (value - high.astype(F32)).astype(BF16)

    def last_contraction():
        total = None
        for part in halves(earlier(2)):
            term = across(low_rows(2), part)
            total = term if total is None else total + term
        for p in range(2):
            for part in halves(acc2[p]):
                total = total + across(low[2, p], part)
        g2[0] = -total

    def ar(b, phase):
        gb, cb, hb, pb, sb, yb, fb = (
            (g0, c0, h0, p0, s0, y0, f0),
            (g1, c1, h1, p1, s1, y1, f1),
            (g2, c2, h2, p2, s2, y2, f2),
        )[b]

        def ds(start, size):
            return pl.ds(pl.multiple_of(start, size), size)

        def copy(n, src, dst, dev):
            return pltpu.make_async_remote_copy(
                src, dst, ar_send.at[b, n], ar_recv.at[b, n], device_id=dev, device_id_type=MESH
            )

        mine = y * 4 + x
        base = 128 * k + 8 * mine
        peers = [(dx, dy) for dx, dy in PLANE]

        def core():
            return [copy(0, gb.at[:, ds(128 * (1 - k), 128)], cb, sib)]

        def over_plane():
            copies = []
            for dx, dy in peers:
                other = (y + dy) % 4 * 4 + (x + dx) % 4
                copies.append(copy(1, hb.at[:, ds(8 * other, 8)], pb.at[mine], at(dx=dx, dy=dy)))
            return copies

        def over_z():
            return [copy(1 + d, sb, yb.at[z], at(dz=d)) for d in (1, 3, 2)]

        def back_plane():
            part = fb.at[:, ds(base, 8)]
            return [copy(5, part, part, at(dx=dx, dy=dy)) for dx, dy in peers]

        def back_core():
            part = fb.at[:, ds(128 * k, 128)]
            return [copy(6, part, part, sib)]

        def plane_wait():
            return [copy(1, hb.at[:, pl.ds(0, 120)], hb.at[:, pl.ds(0, 120)], sib)]

        def back_wait():
            return [copy(5, fb.at[:, pl.ds(0, 120)], fb.at[:, pl.ds(0, 120)], sib)]

        stages = (core, over_plane, over_z, back_plane, back_core)
        waits = (core, plane_wait, over_z, back_wait, back_core)
        if phase > 0:
            for c in waits[phase - 1]():
                c.wait_recv()
        if phase == 1:
            hb[...] = gb[:, ds(128 * k, 128)] + cb[...]
            pb[mine] = hb[:, ds(8 * mine, 8)]
        if phase == 2:
            total = [pb[i] for i in range(16)]
            while len(total) > 1:
                total = [total[i] + total[i + 1] for i in range(0, len(total), 2)]
            sb[...] = total[0]
            yb[z] = total[0]
        if phase == 3:
            fb[:, ds(base, 8)] = (yb[0] + yb[1]) + (yb[2] + yb[3])
        if phase < 5:
            for c in stages[phase]():
                c.start()
        if phase == 5:
            for stage in waits:
                for c in stage():
                    c.wait_send()

    def times(value, factor, turned=False):
        total = None
        for part in halves(value):
            if turned:
                term = across(factor, part)
            else:
                term = jnp.dot(part, factor, preferred_element_type=F32)
            total = term if total is None else total + term
        return total

    pl.semaphore_wait(barrier, len(partners))

    @pl.when(is_src & (k == src_k))
    def _():
        own = piece(own_half, y, 0)
        for t in range(3):
            for s in range(2):
                lo[t][own + s] = low[t, s]
                pltpu.make_async_remote_copy(
                    lo[t].at[own + s], lo[t].at[own + s], lo_send.at[t, 30 + s], lo_recv.at[t, own + s],
                    device_id=sib, device_id_type=MESH,
                ).start()

    @pl.when(is_src & (k != src_k))
    def _():
        own = piece(own_half, y, 0)
        for t in range(3):
            for s in range(2):
                arrived(t, own + s)

    gather_steps(((0, 1), (1, 1), (2, 1)), ())
    found = slot_lists(rows[...], cols[...], count[0, 0], panel_rows, row, z)
    for i in range(3):
        lists[i : i + 1, :] = found[i]
    table_copy = pltpu.make_async_copy(lists, table, local_sem.at[3])
    table_copy.start()
    gather_steps(((0, 2),), ((0, 1),))
    gather_steps(((1, 2), (0, 3)), ((1, 1),))
    gather_steps(((2, 2), (1, 3), (0, 4)), ((2, 1), (0, 2), (0, 3)))
    gather_steps(((2, 3), (1, 4)), ((1, 2), (1, 3)))
    gather_steps(((0, 5), (0, 6)), ())
    from_sibling(0)
    table_copy.wait()
    block_copy.wait()
    multiply(0, 0, 10)
    gather_steps(((2, 4),), ((2, 2), (2, 3)))
    multiply(0, 10, 25)
    rs_first(0)
    gather_steps(((1, 5), (1, 6)), ())
    from_sibling(1)
    multiply(1, 0, 10)
    rs_second(0)
    gather_steps(((2, 5), (2, 6)), ())
    multiply(1, 10, 25)
    rs_first(1)
    new_copy.wait()
    panel(0)
    ar(0, 0)
    from_sibling(2)
    multiply(2, 0, 10)
    rs_second(1)
    ar(0, 1)
    multiply(2, 10, 25)
    rs_first(2)
    panel(1)
    ar(1, 0)
    last_contraction()
    ar(2, 0)
    ar(1, 1)
    ar(2, 1)
    rs_second(2)
    ar(0, 2)
    panel(2)
    ar(1, 2)
    ar(2, 2)
    ar(0, 3)
    ar(1, 3)
    ar(2, 3)
    ar(0, 4)
    ar(0, 5)
    diag_copy.wait()
    y00 = diag[0] - f0[2]
    y10 = -(f0[0] + times(y00, new[1, 0]))
    super_out[0, 0] = y00
    super_out[1, 0] = y10
    ar(1, 4)
    nothing = jnp.zeros((256, 256), F32)
    super_out[0, 1] = nothing
    super_out[0, 2] = nothing
    super_out[1, 2] = nothing
    y20 = -(f0[1] + (times(y00, new[2, 0]) + times(y10, new[2, 1])))
    super_out[2, 0] = y20
    ar(2, 4)
    ar(1, 5)
    y11 = (diag[1] - f1[1]) - times(y10, new[1, 0], True)
    super_out[1, 1] = y11
    y21 = -(f1[0] + (times(y10.T, new[2, 0]) + times(y11, new[2, 1])))
    super_out[2, 1] = y21
    rest = diag[2] - (times(y20, new[2, 0], True) + times(y21, new[2, 1], True))
    ar(2, 5)
    super_out[2, 2] = rest - f2[0]

    for t in range(3):
        for n in range(6):
            rs_copy(t, n).wait_send()

    def send_done(t, n):
        pltpu.make_async_remote_copy(
            lo[t].at[0], lo[t].at[0], lo_send.at[t, n], lo_recv.at[t, 0],
            device_id=sib, device_id_type=MESH,
        ).wait_send()

    @pl.when(is_src & (k == src_k))
    def _():
        for t in range(3):
            for s in range(2):
                send_done(t, 30 + s)

    @pl.when(is_src)
    def _():
        for t, n in sent["src"]:
            send_done(t, n)

    @pl.when(jnp.logical_not(is_src))
    def _():
        for t, n in sent["mid"]:
            send_done(t, n)


def per_device(
    inverse_blocks,
    inverse_rows,
    inverse_cols,
    inverse_count,
    panel_rows,
    lower_old,
    lower_new,
    diag_inverse,
):
    smem = pl.BlockSpec(memory_space=pltpu.SMEM)
    vmem = pl.BlockSpec(memory_space=pltpu.VMEM)
    hbm = pl.BlockSpec(memory_space=pltpu.HBM)

    def each(*shape):
        return [pltpu.VMEM(tuple(nb if s is None else s for s in shape), F32) for nb in BUNDLES]

    return pl.pallas_call(
        kernel,
        out_shape=(
            jax.ShapeDtypeStruct((3, 2, 64, 256), BF16),
            jax.ShapeDtypeStruct((3, 3, 256, 256), F32),
        ),
        in_specs=[vmem, vmem, smem, smem, vmem, hbm, hbm, hbm],
        out_specs=(vmem, vmem),
        scratch_shapes=[
            pltpu.VMEM((3, 128), jnp.int32),
            pltpu.SMEM((3, 128), jnp.int32),
            pltpu.VMEM((97, 256, 256), BF16),
            *[pltpu.VMEM((16, 256, 256), BF16)] * 3,
            *[pltpu.VMEM((2, 256, 256), F32)] * 3,
            pltpu.VMEM((3, 3, 256, 256), BF16),
            pltpu.VMEM((3, 256, 256), F32),
            pltpu.VMEM((3, 64, 256), F32),
            pltpu.VMEM((3, 64, 256), F32),
            pltpu.VMEM((3, 2, 64, 256), F32),
            pltpu.VMEM((3, 2, 64, 256), F32),
            pltpu.VMEM((3, 128, 256), BF16),
            *each(None, 256, 256),
            *each(None, 128, 256),
            *each(None, 128, 256),
            *each(16, None, 8, 256),
            *each(None, 8, 256),
            *each(4, None, 8, 256),
            *each(None, 256, 256),
            pltpu.SemaphoreType.DMA((4,)),
            pltpu.SemaphoreType.DMA((3, 32)),
            pltpu.SemaphoreType.DMA((3, 16)),
            pltpu.SemaphoreType.DMA((3, 6)),
            pltpu.SemaphoreType.DMA((3, 6)),
            pltpu.SemaphoreType.DMA((3, 7)),
            pltpu.SemaphoreType.DMA((3, 7)),
        ],
        compiler_params=pltpu.CompilerParams(
            collective_id=0, has_side_effects=True, vmem_limit_bytes=52 * 2**20
        ),
    )(inverse_rows, inverse_cols, inverse_count, panel_rows, lower_old, inverse_blocks, lower_new, diag_inverse)


def solution(mesh):
    placed = (
        P("row", "col", None, None),
        P("row", "col"),
        P("row", "col"),
        P("row", "col"),
        P(),
        P(None, "row", None, None),
        P(),
        P(),
    )
    return jax.shard_map(
        per_device,
        mesh=mesh,
        in_specs=placed,
        out_specs=(P(None, "row", "col", None), P()),
        check_vma=False,
    )
```

```python
import functools

import jax
import jax.numpy as jnp
from jax import lax
from jax.experimental import pallas as pl
from jax.experimental.pallas import tpu as pltpu
from jax.sharding import PartitionSpec as P

MESH = pl.DeviceIdType.MESH
GROUP = 4
BUNDLES = (3, 2, 1)
PLANE = tuple((dx, dy) for dy in (1, 3, 0, 2) for dx in (1, 3, 0, 2) if (dx, dy) != (0, 0))
F32 = jnp.float32
BF16 = jnp.bfloat16


def slot_lists(rows, cols, count, panel_rows, row, col):
    kmax = rows.shape[1]
    slot = lax.broadcasted_iota(jnp.int32, (kmax, kmax), 0)
    other = lax.broadcasted_iota(jnp.int32, (kmax, kmax), 1)

    def upright(line):
        return jnp.sum(jnp.where(slot == other, jnp.broadcast_to(line, (kmax, kmax)), 0), axis=1, keepdims=True)

    stored_row, stored_col = upright(rows), upright(cols)
    index = lax.broadcasted_iota(jnp.int32, (kmax, 1), 0)
    live = index < count
    useful = jnp.zeros((kmax, 1), jnp.int32)
    position = jnp.zeros((kmax, 1), jnp.int32)
    for i in range(8):
        for j in range(2):
            same = stored_col == panel_rows[(i * 4 + col) * 2 + j]
            useful = jnp.where(same & live, 1, useful)
            position = jnp.where(same, i * 2 + j, position)
    mine = [jnp.where(stored_row == panel_rows[row * 2 + p], useful, 0) for p in range(2)]
    flat = [jnp.sum(jnp.where(slot == other, jnp.broadcast_to(m, (kmax, kmax)), 0), axis=0, keepdims=True) for m in mine]
    rank = [
        jnp.sum(jnp.where(other < slot, jnp.broadcast_to(f, (kmax, kmax)), 0), axis=1, keepdims=True) for f in flat
    ]
    first = jnp.sum(jnp.broadcast_to(flat[0], (8, kmax)), axis=1, keepdims=True)[0:1]
    padding = jnp.where(first % GROUP == 0, 0, GROUP - first % GROUP)
    start = first + padding
    place = jnp.where(mine[0] == 1, rank[0], jnp.where(mine[1] == 1, start + rank[1], -1))
    hit = place == lax.broadcasted_iota(jnp.int32, (kmax, 128), 1)
    filled = jnp.sum(jnp.where(hit, 1, 0), axis=0, keepdims=True)
    slot_at = jnp.sum(jnp.where(hit, index, 0), axis=0, keepdims=True)
    cand_at = jnp.sum(jnp.where(hit, position, 0), axis=0, keepdims=True)
    lane = lax.broadcasted_iota(jnp.int32, (1, 128), 1)
    is_first = jnp.where(lane * GROUP < start, 1, 0)
    return jnp.where(filled == 1, slot_at, kmax), cand_at, is_first


def kernel(
    rows_hbm, cols_hbm, count_hbm, panel_hbm, low_hbm, blocks_hbm, new_hbm, diag_hbm,
    panel_out, super_out,
    rows, cols, count, panel_rows, low, lists, table,
    blocks, lo0, lo1, lo2, acc0, acc1, acc2, new, diag,
    rs_a, rs_b, rs_p, rs_m, u_all, low_t, v_high, v_low,
    g0, g1, g2, c0, c1, c2, h0, h1, h2, p0, p1, p2, s0, s1, s2, y0, y1, y2, f0, f1, f2,
    local_sem, lo_send, lo_recv, rs_send, rs_recv, ar_send, ar_recv,
):
    lo = (lo0, lo1, lo2)
    acc = (acc0, acc1, acc2)
    row = lax.axis_index("row")
    z = lax.axis_index("col")
    y = row // 8
    x = (row // 2) % 4
    k = row % 2
    sib = (y * 8 + x * 2 + (1 - k), z)

    def at(dx=0, dy=0, dz=0):
        return ((y + dy + 4) % 4 * 8 + (x + dx + 4) % 4 * 2 + k, (z + dz + 4) % 4)

    barrier = pltpu.get_barrier_semaphore()
    partners = [sib]
    partners += [at(dx=dx, dy=dy) for dx, dy in PLANE]
    partners += [at(dz=d) for d in (1, 2, 3)]
    for dev in partners:
        pl.semaphore_signal(barrier, inc=1, device_id=dev, device_id_type=MESH)

    block_copy = pltpu.make_async_copy(blocks_hbm.at[0], blocks.at[pl.ds(0, 96)], local_sem.at[0])
    new_copy = pltpu.make_async_copy(new_hbm, new, local_sem.at[1])
    diag_copy = pltpu.make_async_copy(diag_hbm, diag, local_sem.at[2])
    low_copy = pltpu.make_async_copy(low_hbm, low, local_sem.at[4])
    index_copies = [
        pltpu.make_async_copy(src, dst, local_sem.at[5 + i])
        for i, (src, dst) in enumerate(
            ((rows_hbm, rows), (cols_hbm, cols), (count_hbm, count), (panel_hbm, panel_rows))
        )
    ]
    low_copy.start()
    for c in index_copies:
        c.start()
    block_copy.start()
    new_copy.start()
    diag_copy.start()
    blocks[96] = jnp.zeros((256, 256), BF16)

    src_x = z // 2
    src_k = z % 2
    is_src = x % 2 == src_x
    def piece(half, yy, slot):
        return ((yy + 8) % 4 * 2 + half) * 2 + slot

    own_half = x // 2
    left_half = (x + 3) % 4 // 2
    right_half = (x + 1) % 4 // 2
    far_half = 1 - own_half

    sent = {"src": [], "mid": []}

    def send(role, t, cand, dev):
        n = len([1 for (tt, _) in sent[role] if tt == t])
        sent[role].append((t, n))
        pltpu.make_async_remote_copy(
            lo[t].at[cand], lo[t].at[cand], lo_send.at[t, n], lo_recv.at[t, cand],
            device_id=dev, device_id_type=MESH,
        ).start()

    def arrived(t, cand):
        pltpu.make_async_remote_copy(
            lo[t].at[cand], lo[t].at[cand], lo_send.at[t, 0], lo_recv.at[t, cand],
            device_id=sib, device_id_type=MESH,
        ).wait_recv()

    def src_step(t, step):
        if step == 1:
            own = piece(own_half, y, k)
            for dev in (at(dx=1), at(dx=-1), at(dy=1), at(dy=-1), at(dy=2)):
                send("src", t, own, dev)
        if step == 2:
            for d in (1, 3):
                c = piece(own_half, y + d, k)
                arrived(t, c)
                send("src", t, c, sib)
        if step == 3:
            c = piece(own_half, y + 2, k)
            arrived(t, c)
            send("src", t, c, at(dx=1))
            send("src", t, c, at(dx=-1))
            send("src", t, c, sib)
        if step >= 4:
            for d in {4: (0,), 5: (1, 3), 6: (2,)}[step]:
                c = piece(far_half, y + d, k)
                arrived(t, c)
                send("src", t, c, sib)

    def mid_step(t, step):
        for d in {1: (0,), 2: (3, 1), 3: (2,)}[step]:
            c = piece(left_half, y + d, k)
            arrived(t, c)
            if d == 0:
                send("mid", t, c, at(dy=1))
                send("mid", t, c, at(dy=-1))
            if d in (0, 1):
                send("mid", t, c, at(dx=1))
            send("mid", t, c, sib)
            c = piece(right_half, y + d, k)
            arrived(t, c)
            if d == 0:
                send("mid", t, c, at(dy=1))
                send("mid", t, c, at(dy=-1))
            if d in (2, 3):
                send("mid", t, c, at(dx=-1))
            send("mid", t, c, sib)

    def gather_steps(src_steps, mid_steps):
        @pl.when(is_src)
        def _():
            for t, step in src_steps:
                src_step(t, step)

        @pl.when(jnp.logical_not(is_src))
        def _():
            for t, step in mid_steps:
                mid_step(t, step)

    def from_sibling(t):
        @pl.when(is_src)
        def _():
            for d in (1, 2, 3):
                arrived(t, piece(own_half, y + d, 1 - k))
            for d in range(4):
                arrived(t, piece(far_half, y + d, 1 - k))

        @pl.when(jnp.logical_not(is_src))
        def _():
            for d in range(4):
                arrived(t, piece(left_half, y + d, 1 - k))
                arrived(t, piece(right_half, y + d, 1 - k))

    def multiply(t, begin, end):
        if begin == 0:
            acc[t][...] = jnp.zeros((2, 256, 256), F32)

        def body(g, carry):
            left = [blocks[table[0, g * GROUP + i]] for i in range(GROUP)]
            right = [lo[t][table[1, g * GROUP + i]] for i in range(GROUP)]
            product = jnp.dot(
                jnp.concatenate(left, axis=1), jnp.concatenate(right, axis=0), preferred_element_type=F32
            )
            weight = table[2, g].astype(F32)
            acc[t][0] += product * weight
            acc[t][1] += product * (1.0 - weight)
            return carry

        lax.fori_loop(begin, end, body, 0, unroll=5)

    def quarter(d):
        return pl.ds(pl.multiple_of((z + d) % 4 * 64, 64), 64)

    def rs_copy(t, n):
        a = acc[t]
        src, dst, dev = (
            (a.at[0, quarter(2)], rs_a.at[t], at(dz=1)),
            (a.at[1, quarter(2)], rs_b.at[t], at(dz=3)),
            (a.at[1, quarter(1)], rs_p.at[t, 1], at(dz=1)),
            (a.at[0, quarter(3)], rs_m.at[t, 0], at(dz=3)),
            (a.at[0, quarter(1)], rs_p.at[t, 0], at(dz=1)),
            (a.at[1, quarter(3)], rs_m.at[t, 1], at(dz=3)),
        )[n]
        return pltpu.make_async_remote_copy(
            src, dst, rs_send.at[t, n], rs_recv.at[t, n], device_id=dev, device_id_type=MESH
        )

    def rs_first(t):
        for n in range(4):
            rs_copy(t, n).start()

    def rs_second(t):
        rs_copy(t, 0).wait_recv()
        acc[t][0, quarter(1)] += rs_a[t]
        rs_copy(t, 4).start()
        rs_copy(t, 1).wait_recv()
        acc[t][1, quarter(3)] += rs_b[t]
        rs_copy(t, 5).start()

    def rs_third(t):
        for n in (2, 3, 4, 5):
            rs_copy(t, n).wait_recv()
        return (acc[t][:, quarter(0)] + (rs_p[t] + rs_m[t])).reshape(128, 256)

    def across(left, right):
        return lax.dot_general(left, right, (((0,), (0,)), ((), ())), preferred_element_type=F32)

    g = (g0, g1, g2)

    def panel(t):
        running = rs_third(t)
        for e in range(t):
            running = running + jnp.dot(u_all[e], new[t, e], preferred_element_type=F32)
        current = (-running).astype(BF16)
        u_all[t] = current
        panel_out[t] = current.reshape(2, 64, 256)

    def halves(value):
        high = value.astype(BF16)
        return high, (value - high.astype(F32)).astype(BF16)

    def turn_low():
        for t in range(3):
            low_t[t] = low[t].reshape(512, 256).T

    def contract(t):
        for p in range(2):
            rows_p = pl.ds(256 * p, 256)
            value = acc[t][p]
            for e in range(t):
                for part in (v_low, v_high):
                    value = value + jnp.dot(part[e, rows_p], new[t, e], preferred_element_type=F32)
            v_high[t, rows_p], v_low[t, rows_p] = halves(-value)
        for i, other in enumerate({0: (1, 2, 0), 1: (2, 1), 2: (2,)}[t]):
            g[t][i] = jnp.dot(low_t[other], v_low[t], preferred_element_type=F32) + jnp.dot(
                low_t[other], v_high[t], preferred_element_type=F32
            )

    def ar(b, phase):
        gb, cb, hb, pb, sb, yb, fb = (
            (g0, c0, h0, p0, s0, y0, f0),
            (g1, c1, h1, p1, s1, y1, f1),
            (g2, c2, h2, p2, s2, y2, f2),
        )[b]

        def ds(start, size):
            return pl.ds(pl.multiple_of(start, size), size)

        def copy(n, src, dst, dev):
            return pltpu.make_async_remote_copy(
                src, dst, ar_send.at[b, n], ar_recv.at[b, n], device_id=dev, device_id_type=MESH
            )

        mine = y * 4 + x
        base = 128 * k + 8 * mine
        peers = [(dx, dy) for dx, dy in PLANE]

        def core():
            return [copy(0, gb.at[:, ds(128 * (1 - k), 128)], cb, sib)]

        def over_plane():
            copies = []
            for dx, dy in peers:
                other = (y + dy) % 4 * 4 + (x + dx) % 4
                copies.append(copy(1, hb.at[:, ds(8 * other, 8)], pb.at[mine], at(dx=dx, dy=dy)))
            return copies

        def over_z():
            return [copy(1 + d, sb, yb.at[z], at(dz=d)) for d in (1, 3, 2)]

        def back_plane():
            part = fb.at[:, ds(base, 8)]
            return [copy(5, part, part, at(dx=dx, dy=dy)) for dx, dy in peers]

        def back_core():
            part = fb.at[:, ds(128 * k, 128)]
            return [copy(6, part, part, sib)]

        def plane_wait():
            return [copy(1, hb.at[:, pl.ds(0, 120)], hb.at[:, pl.ds(0, 120)], sib)]

        def back_wait():
            return [copy(5, fb.at[:, pl.ds(0, 120)], fb.at[:, pl.ds(0, 120)], sib)]

        stages = (core, over_plane, over_z, back_plane, back_core)
        waits = (core, plane_wait, over_z, back_wait, back_core)
        if phase > 0:
            for c in waits[phase - 1]():
                c.wait_recv()
        if phase == 1:
            hb[...] = gb[:, ds(128 * k, 128)] + cb[...]
            pb[mine] = hb[:, ds(8 * mine, 8)]
        if phase == 2:
            total = [pb[i] for i in range(16)]
            while len(total) > 1:
                total = [total[i] + total[i + 1] for i in range(0, len(total), 2)]
            sb[...] = total[0]
            yb[z] = total[0]
        if phase == 3:
            fb[:, ds(base, 8)] = (yb[0] + yb[1]) + (yb[2] + yb[3])
        if phase < 5:
            for c in stages[phase]():
                c.start()
        if phase == 5:
            for stage in waits:
                for c in stage():
                    c.wait_send()

    def times(value, factor, turned=False):
        total = None
        for part in halves(value):
            if turned:
                term = across(factor, part)
            else:
                term = jnp.dot(part, factor, preferred_element_type=F32)
            total = term if total is None else total + term
        return total

    low_copy.wait()
    pl.semaphore_wait(barrier, len(partners))

    @pl.when(is_src & (k == src_k))
    def _():
        own = piece(own_half, y, 0)
        for t in range(3):
            for s in range(2):
                lo[t][own + s] = low[t, s]
                pltpu.make_async_remote_copy(
                    lo[t].at[own + s], lo[t].at[own + s], lo_send.at[t, 30 + s], lo_recv.at[t, own + s],
                    device_id=sib, device_id_type=MESH,
                ).start()

    @pl.when(is_src & (k != src_k))
    def _():
        own = piece(own_half, y, 0)
        for t in range(3):
            for s in range(2):
                arrived(t, own + s)

    gather_steps(((0, 1), (1, 1), (2, 1)), ())
    for c in index_copies:
        c.wait()
    found = slot_lists(rows[...], cols[...], count[0, 0], panel_rows, row, z)
    for i in range(3):
        lists[i : i + 1, :] = found[i]
    table_copy = pltpu.make_async_copy(lists, table, local_sem.at[3])
    table_copy.start()
    turn_low()
    new_copy.wait()
    gather_steps(((0, 2),), ((0, 1),))
    gather_steps(((1, 2), (0, 3)), ((1, 1),))
    gather_steps(((2, 2), (1, 3), (0, 4)), ((2, 1), (0, 2), (0, 3)))
    gather_steps(((2, 3), (1, 4)), ((1, 2), (1, 3)))
    gather_steps(((0, 5), (0, 6)), ())
    from_sibling(0)
    table_copy.wait()
    block_copy.wait()
    multiply(0, 0, 25)
    rs_first(0)
    contract(0)
    ar(0, 0)
    gather_steps(((2, 4), (1, 5), (1, 6)), ((2, 2),))
    from_sibling(1)
    ar(0, 1)
    multiply(1, 0, 15)
    gather_steps((), ((2, 3),))
    multiply(1, 15, 25)
    rs_first(1)
    contract(1)
    ar(1, 0)
    gather_steps(((2, 5), (2, 6)), ())
    rs_second(0)
    ar(0, 2)
    ar(1, 1)
    from_sibling(2)
    multiply(2, 0, 25)
    rs_first(2)
    contract(2)
    ar(2, 0)
    ar(0, 3)
    ar(2, 1)
    rs_second(1)
    ar(1, 2)
    panel(0)
    rs_second(2)
    ar(2, 2)
    ar(1, 3)
    ar(0, 4)
    panel(1)
    ar(2, 3)
    ar(0, 5)
    diag_copy.wait()
    y00 = diag[0] - f0[2]
    y10 = -(f0[0].T + times(y00, new[1, 0]))
    super_out[0] = y00
    super_out[1] = y10
    ar(1, 4)
    y20 = -(f0[1].T + (times(y00, new[2, 0]) + times(y10, new[2, 1])))
    super_out[3] = y20
    ar(2, 4)
    ar(1, 5)
    panel(2)
    y11 = (diag[1] - f1[1]) - times(y10, new[1, 0], True)
    super_out[2] = y11
    y21 = -(f1[0].T + (times(y10.T, new[2, 0]) + times(y11, new[2, 1])))
    super_out[4] = y21
    rest = diag[2] - (times(y20, new[2, 0], True) + times(y21, new[2, 1], True))
    ar(2, 5)
    super_out[5] = rest - f2[0]

    for t in range(3):
        for n in range(6):
            rs_copy(t, n).wait_send()

    def send_done(t, n):
        pltpu.make_async_remote_copy(
            lo[t].at[0], lo[t].at[0], lo_send.at[t, n], lo_recv.at[t, 0],
            device_id=sib, device_id_type=MESH,
        ).wait_send()

    @pl.when(is_src & (k == src_k))
    def _():
        for t in range(3):
            for s in range(2):
                send_done(t, 30 + s)

    @pl.when(is_src)
    def _():
        for t, n in sent["src"]:
            send_done(t, n)

    @pl.when(jnp.logical_not(is_src))
    def _():
        for t, n in sent["mid"]:
            send_done(t, n)


def place_kernel(found, out):
    for i in range(3):
        for j in range(3):
            out[i, j] = found[i * (i + 1) // 2 + j] if j <= i else jnp.zeros((256, 256), F32)


def per_device(
    inverse_blocks,
    inverse_rows,
    inverse_cols,
    inverse_count,
    panel_rows,
    lower_old,
    lower_new,
    diag_inverse,
):
    vmem = pl.BlockSpec(memory_space=pltpu.VMEM)
    hbm = pl.BlockSpec(memory_space=pltpu.HBM)

    def each(*shape):
        return [pltpu.VMEM(tuple(nb if s is None else s for s in shape), F32) for nb in BUNDLES]

    panels, found = pl.pallas_call(
        kernel,
        out_shape=(
            jax.ShapeDtypeStruct((3, 2, 64, 256), BF16),
            jax.ShapeDtypeStruct((6, 256, 256), F32),
        ),
        in_specs=[hbm] * 8,
        out_specs=(vmem, vmem),
        scratch_shapes=[
            pltpu.VMEM((1, 96), jnp.int32),
            pltpu.VMEM((1, 96), jnp.int32),
            pltpu.SMEM((1, 1), jnp.int32),
            pltpu.SMEM((64,), jnp.int32),
            pltpu.VMEM((3, 2, 256, 256), BF16),
            pltpu.VMEM((3, 128), jnp.int32),
            pltpu.SMEM((3, 128), jnp.int32),
            pltpu.VMEM((97, 256, 256), BF16),
            *[pltpu.VMEM((16, 256, 256), BF16)] * 3,
            *[pltpu.VMEM((2, 256, 256), F32)] * 3,
            pltpu.VMEM((3, 3, 256, 256), BF16),
            pltpu.VMEM((3, 256, 256), F32),
            pltpu.VMEM((3, 64, 256), F32),
            pltpu.VMEM((3, 64, 256), F32),
            pltpu.VMEM((3, 2, 64, 256), F32),
            pltpu.VMEM((3, 2, 64, 256), F32),
            pltpu.VMEM((3, 128, 256), BF16),
            pltpu.VMEM((3, 256, 512), BF16),
            pltpu.VMEM((3, 512, 256), BF16),
            pltpu.VMEM((3, 512, 256), BF16),
            *each(None, 256, 256),
            *each(None, 128, 256),
            *each(None, 128, 256),
            *each(16, None, 8, 256),
            *each(None, 8, 256),
            *each(4, None, 8, 256),
            *each(None, 256, 256),
            pltpu.SemaphoreType.DMA((9,)),
            pltpu.SemaphoreType.DMA((3, 32)),
            pltpu.SemaphoreType.DMA((3, 16)),
            pltpu.SemaphoreType.DMA((3, 6)),
            pltpu.SemaphoreType.DMA((3, 6)),
            pltpu.SemaphoreType.DMA((3, 7)),
            pltpu.SemaphoreType.DMA((3, 7)),
        ],
        compiler_params=pltpu.CompilerParams(
            collective_id=0, has_side_effects=True, vmem_limit_bytes=60 * 2**20
        ),
    )(inverse_rows, inverse_cols, inverse_count, panel_rows, lower_old, inverse_blocks, lower_new, diag_inverse)
    placed = pl.pallas_call(
        place_kernel,
        out_shape=jax.ShapeDtypeStruct((3, 3, 256, 256), F32),
        in_specs=[vmem],
        out_specs=vmem,
    )(found)
    return panels, placed


def solution(mesh):
    placed = (
        P("row", "col", None, None),
        P("row", "col"),
        P("row", "col"),
        P("row", "col"),
        P(),
        P(None, "row", None, None),
        P(),
        P(),
    )
    return jax.shard_map(
        per_device,
        mesh=mesh,
        in_specs=placed,
        out_specs=(P(None, "row", "col", None), P()),
        check_vma=False,
    )
```

```python
import functools

import jax
import jax.numpy as jnp
from jax import lax
from jax.experimental import pallas as pl
from jax.experimental.pallas import tpu as pltpu
from jax.sharding import PartitionSpec as P

MESH = pl.DeviceIdType.MESH
GROUP = 4
BUNDLES = (3, 2, 1)
PLANE = tuple((dx, dy) for dy in (1, 3, 0, 2) for dx in (1, 3, 0, 2) if (dx, dy) != (0, 0))
F32 = jnp.float32
BF16 = jnp.bfloat16


def slot_lists(rows, cols, count, panel_rows, row, col):
    kmax = rows.shape[1]
    slot = lax.broadcasted_iota(jnp.int32, (kmax, kmax), 0)
    other = lax.broadcasted_iota(jnp.int32, (kmax, kmax), 1)

    def upright(line):
        return jnp.sum(jnp.where(slot == other, jnp.broadcast_to(line, (kmax, kmax)), 0), axis=1, keepdims=True)

    stored_row, stored_col = upright(rows), upright(cols)
    index = lax.broadcasted_iota(jnp.int32, (kmax, 1), 0)
    live = index < count
    useful = jnp.zeros((kmax, 1), jnp.int32)
    position = jnp.zeros((kmax, 1), jnp.int32)
    for i in range(8):
        for j in range(2):
            same = stored_col == panel_rows[(i * 4 + col) * 2 + j]
            useful = jnp.where(same & live, 1, useful)
            position = jnp.where(same, i * 2 + j, position)
    mine = [jnp.where(stored_row == panel_rows[row * 2 + p], useful, 0) for p in range(2)]
    flat = [jnp.sum(jnp.where(slot == other, jnp.broadcast_to(m, (kmax, kmax)), 0), axis=0, keepdims=True) for m in mine]
    rank = [
        jnp.sum(jnp.where(other < slot, jnp.broadcast_to(f, (kmax, kmax)), 0), axis=1, keepdims=True) for f in flat
    ]
    first = jnp.sum(jnp.broadcast_to(flat[0], (8, kmax)), axis=1, keepdims=True)[0:1]
    padding = jnp.where(first % GROUP == 0, 0, GROUP - first % GROUP)
    start = first + padding
    place = jnp.where(mine[0] == 1, rank[0], jnp.where(mine[1] == 1, start + rank[1], -1))
    hit = place == lax.broadcasted_iota(jnp.int32, (kmax, 128), 1)
    filled = jnp.sum(jnp.where(hit, 1, 0), axis=0, keepdims=True)
    slot_at = jnp.sum(jnp.where(hit, index, 0), axis=0, keepdims=True)
    cand_at = jnp.sum(jnp.where(hit, position, 0), axis=0, keepdims=True)
    lane = lax.broadcasted_iota(jnp.int32, (1, 128), 1)
    is_first = jnp.where(lane * GROUP < start, 1, 0)
    return jnp.where(filled == 1, slot_at, kmax), cand_at, is_first


def kernel(
    rows_hbm, cols_hbm, count_hbm, panel_hbm, low_hbm, blocks_hbm, new_hbm, diag_hbm,
    panel_out, super_out,
    rows, cols, count, panel_rows, low, lists, table,
    blocks, lo0, lo1, lo2, acc0, acc1, acc2, new, diag,
    rs_a, rs_b, rs_p, rs_m, u_all, low_t, v_high, v_low,
    g0, g1, g2, c0, c1, c2, h0, h1, h2, p0, p1, p2, s0, s1, s2, y0, y1, y2, f0, f1, f2,
    local_sem, lo_send, lo_recv, rs_send, rs_recv, ar_send, ar_recv,
):
    lo = (lo0, lo1, lo2)
    acc = (acc0, acc1, acc2)
    row = lax.axis_index("row")
    z = lax.axis_index("col")
    y = row // 8
    x = (row // 2) % 4
    k = row % 2
    sib = (y * 8 + x * 2 + (1 - k), z)

    def at(dx=0, dy=0, dz=0):
        return ((y + dy + 4) % 4 * 8 + (x + dx + 4) % 4 * 2 + k, (z + dz + 4) % 4)

    barrier = pltpu.get_barrier_semaphore()
    partners = [sib]
    partners += [at(dx=dx, dy=dy) for dx, dy in PLANE]
    partners += [at(dz=d) for d in (1, 2, 3)]
    for dev in partners:
        pl.semaphore_signal(barrier, inc=1, device_id=dev, device_id_type=MESH)

    block_copy = pltpu.make_async_copy(blocks_hbm.at[0], blocks.at[pl.ds(0, 96)], local_sem.at[0])
    new_copy = pltpu.make_async_copy(new_hbm, new, local_sem.at[1])
    diag_copy = pltpu.make_async_copy(diag_hbm, diag, local_sem.at[2])
    low_copy = pltpu.make_async_copy(low_hbm, low, local_sem.at[4])
    index_copies = [
        pltpu.make_async_copy(src, dst, local_sem.at[5 + i])
        for i, (src, dst) in enumerate(
            ((rows_hbm, rows), (cols_hbm, cols), (count_hbm, count), (panel_hbm, panel_rows))
        )
    ]
    low_copy.start()
    for c in index_copies:
        c.start()
    block_copy.start()
    new_copy.start()
    diag_copy.start()
    blocks[96] = jnp.zeros((256, 256), BF16)

    src_x = z // 2
    src_k = z % 2
    is_src = x % 2 == src_x
    def piece(half, yy, slot):
        return ((yy + 8) % 4 * 2 + half) * 2 + slot

    own_half = x // 2
    left_half = (x + 3) % 4 // 2
    right_half = (x + 1) % 4 // 2
    far_half = 1 - own_half

    sent = {"src": [], "mid": []}

    def send(role, t, cand, dev):
        n = len([1 for (tt, _) in sent[role] if tt == t])
        sent[role].append((t, n))
        pltpu.make_async_remote_copy(
            lo[t].at[cand], lo[t].at[cand], lo_send.at[t, n], lo_recv.at[t, cand],
            device_id=dev, device_id_type=MESH,
        ).start()

    def arrived(t, cand):
        pltpu.make_async_remote_copy(
            lo[t].at[cand], lo[t].at[cand], lo_send.at[t, 0], lo_recv.at[t, cand],
            device_id=sib, device_id_type=MESH,
        ).wait_recv()

    def src_step(t, step):
        if step == 1:
            own = piece(own_half, y, k)
            for dev in (at(dx=1), at(dx=-1), at(dy=1), at(dy=-1), at(dy=2)):
                send("src", t, own, dev)
        if step == 2:
            for d in (1, 3):
                c = piece(own_half, y + d, k)
                arrived(t, c)
                send("src", t, c, sib)
        if step == 3:
            c = piece(own_half, y + 2, k)
            arrived(t, c)
            send("src", t, c, at(dx=1))
            send("src", t, c, at(dx=-1))
            send("src", t, c, sib)
        if step >= 4:
            for d in {4: (0,), 5: (1, 3), 6: (2,)}[step]:
                c = piece(far_half, y + d, k)
                arrived(t, c)
                send("src", t, c, sib)

    def mid_step(t, step):
        for d in {1: (0,), 2: (3, 1), 3: (2,)}[step]:
            c = piece(left_half, y + d, k)
            arrived(t, c)
            if d == 0:
                send("mid", t, c, at(dy=1))
                send("mid", t, c, at(dy=-1))
            if d in (0, 1):
                send("mid", t, c, at(dx=1))
            send("mid", t, c, sib)
            c = piece(right_half, y + d, k)
            arrived(t, c)
            if d == 0:
                send("mid", t, c, at(dy=1))
                send("mid", t, c, at(dy=-1))
            if d in (2, 3):
                send("mid", t, c, at(dx=-1))
            send("mid", t, c, sib)

    def gather_steps(src_steps, mid_steps):
        @pl.when(is_src)
        def _():
            for t, step in src_steps:
                src_step(t, step)

        @pl.when(jnp.logical_not(is_src))
        def _():
            for t, step in mid_steps:
                mid_step(t, step)

    def from_sibling(t):
        @pl.when(is_src)
        def _():
            for d in (1, 2, 3):
                arrived(t, piece(own_half, y + d, 1 - k))
            for d in range(4):
                arrived(t, piece(far_half, y + d, 1 - k))

        @pl.when(jnp.logical_not(is_src))
        def _():
            for d in range(4):
                arrived(t, piece(left_half, y + d, 1 - k))
                arrived(t, piece(right_half, y + d, 1 - k))

    def multiply(t, begin, end):
        if begin == 0:
            acc[t][...] = jnp.zeros((2, 256, 256), F32)

        def body(g, carry):
            left = [blocks[table[0, g * GROUP + i]] for i in range(GROUP)]
            right = [lo[t][table[1, g * GROUP + i]] for i in range(GROUP)]
            product = jnp.dot(
                jnp.concatenate(left, axis=1), jnp.concatenate(right, axis=0), preferred_element_type=F32
            )
            weight = table[2, g].astype(F32)
            acc[t][0] += product * weight
            acc[t][1] += product * (1.0 - weight)
            return carry

        lax.fori_loop(begin, end, body, 0, unroll=5)

    def quarter(d):
        return pl.ds(pl.multiple_of((z + d) % 4 * 64, 64), 64)

    def rs_copy(t, n):
        a = acc[t]
        src, dst, dev = (
            (a.at[0, quarter(2)], rs_a.at[t], at(dz=1)),
            (a.at[1, quarter(2)], rs_b.at[t], at(dz=3)),
            (a.at[1, quarter(1)], rs_p.at[t, 1], at(dz=1)),
            (a.at[0, quarter(3)], rs_m.at[t, 0], at(dz=3)),
            (a.at[0, quarter(1)], rs_p.at[t, 0], at(dz=1)),
            (a.at[1, quarter(3)], rs_m.at[t, 1], at(dz=3)),
        )[n]
        return pltpu.make_async_remote_copy(
            src, dst, rs_send.at[t, n], rs_recv.at[t, n], device_id=dev, device_id_type=MESH
        )

    def rs_first(t):
        for n in range(4):
            rs_copy(t, n).start()

    def rs_second(t):
        rs_copy(t, 0).wait_recv()
        acc[t][0, quarter(1)] += rs_a[t]
        rs_copy(t, 4).start()
        rs_copy(t, 1).wait_recv()
        acc[t][1, quarter(3)] += rs_b[t]
        rs_copy(t, 5).start()

    def rs_third(t):
        for n in (2, 3, 4, 5):
            rs_copy(t, n).wait_recv()
        return (acc[t][:, quarter(0)] + (rs_p[t] + rs_m[t])).reshape(128, 256)

    def across(left, right):
        return lax.dot_general(left, right, (((0,), (0,)), ((), ())), preferred_element_type=F32)

    g = (g0, g1, g2)

    def panel(t):
        running = rs_third(t)
        for e in range(t):
            running = running + jnp.dot(u_all[e], new[t, e], preferred_element_type=F32)
        current = (-running).astype(BF16)
        u_all[t] = current
        panel_out[t] = current.reshape(2, 64, 256)

    def halves(value):
        high = value.astype(BF16)
        return high, (value - high.astype(F32)).astype(BF16)

    def turn_low():
        for t in range(3):
            low_t[t] = low[t].reshape(512, 256).T

    def contract(t):
        for p in range(2):
            rows_p = pl.ds(256 * p, 256)
            value = acc[t][p]
            for e in range(t):
                for part in (v_low, v_high):
                    value = value + jnp.dot(part[e, rows_p], new[t, e], preferred_element_type=F32)
            v_high[t, rows_p], v_low[t, rows_p] = halves(-value)
        for i, other in enumerate({0: (1, 2, 0), 1: (2, 1), 2: (2,)}[t]):
            g[t][i] = jnp.dot(low_t[other], v_low[t], preferred_element_type=F32) + jnp.dot(
                low_t[other], v_high[t], preferred_element_type=F32
            )

    def ar(b, phase):
        gb, cb, hb, pb, sb, yb, fb = (
            (g0, c0, h0, p0, s0, y0, f0),
            (g1, c1, h1, p1, s1, y1, f1),
            (g2, c2, h2, p2, s2, y2, f2),
        )[b]

        def ds(start, size):
            return pl.ds(pl.multiple_of(start, size), size)

        def copy(n, src, dst, dev):
            return pltpu.make_async_remote_copy(
                src, dst, ar_send.at[b, n], ar_recv.at[b, n], device_id=dev, device_id_type=MESH
            )

        mine = y * 4 + x
        base = 128 * k + 8 * mine
        peers = [(dx, dy) for dx, dy in PLANE]

        def core():
            return [copy(0, gb.at[:, ds(128 * (1 - k), 128)], cb, sib)]

        def over_plane():
            copies = []
            for dx, dy in peers:
                other = (y + dy) % 4 * 4 + (x + dx) % 4
                copies.append(copy(1, hb.at[:, ds(8 * other, 8)], pb.at[mine], at(dx=dx, dy=dy)))
            return copies

        def over_z():
            return [copy(1 + d, sb, yb.at[z], at(dz=d)) for d in (1, 3, 2)]

        def back_plane():
            part = fb.at[:, ds(base, 8)]
            return [copy(5, part, part, at(dx=dx, dy=dy)) for dx, dy in peers]

        def back_core():
            part = fb.at[:, ds(128 * k, 128)]
            return [copy(6, part, part, sib)]

        def plane_wait():
            return [copy(1, hb.at[:, pl.ds(0, 120)], hb.at[:, pl.ds(0, 120)], sib)]

        def back_wait():
            return [copy(5, fb.at[:, pl.ds(0, 120)], fb.at[:, pl.ds(0, 120)], sib)]

        stages = (core, over_plane, over_z, back_plane, back_core)
        waits = (core, plane_wait, over_z, back_wait, back_core)
        if phase > 0:
            for c in waits[phase - 1]():
                c.wait_recv()
        if phase == 1:
            hb[...] = gb[:, ds(128 * k, 128)] + cb[...]
            pb[mine] = hb[:, ds(8 * mine, 8)]
        if phase == 2:
            total = [pb[i] for i in range(16)]
            while len(total) > 1:
                total = [total[i] + total[i + 1] for i in range(0, len(total), 2)]
            sb[...] = total[0]
            yb[z] = total[0]
        if phase == 3:
            fb[:, ds(base, 8)] = (yb[0] + yb[1]) + (yb[2] + yb[3])
        if phase < 5:
            for c in stages[phase]():
                c.start()
        if phase == 5:
            for stage in waits:
                for c in stage():
                    c.wait_send()

    def times(value, factor, turned=False):
        total = None
        for part in halves(value):
            if turned:
                term = across(factor, part)
            else:
                term = jnp.dot(part, factor, preferred_element_type=F32)
            total = term if total is None else total + term
        return total

    low_copy.wait()
    pl.semaphore_wait(barrier, len(partners))

    @pl.when(is_src & (k == src_k))
    def _():
        own = piece(own_half, y, 0)
        for t in range(3):
            for s in range(2):
                lo[t][own + s] = low[t, s]
                pltpu.make_async_remote_copy(
                    lo[t].at[own + s], lo[t].at[own + s], lo_send.at[t, 30 + s], lo_recv.at[t, own + s],
                    device_id=sib, device_id_type=MESH,
                ).start()

    @pl.when(is_src & (k != src_k))
    def _():
        own = piece(own_half, y, 0)
        for t in range(3):
            for s in range(2):
                arrived(t, own + s)

    gather_steps(((0, 1), (1, 1), (2, 1)), ())
    for c in index_copies:
        c.wait()
    found = slot_lists(rows[...], cols[...], count[0, 0], panel_rows, row, z)
    for i in range(3):
        lists[i : i + 1, :] = found[i]
    table_copy = pltpu.make_async_copy(lists, table, local_sem.at[3])
    table_copy.start()
    turn_low()
    new_copy.wait()
    gather_steps(((0, 2),), ((0, 1),))
    gather_steps(((1, 2), (0, 3)), ((1, 1),))
    gather_steps(((2, 2), (1, 3), (0, 4)), ((2, 1), (0, 2), (0, 3)))
    gather_steps(((2, 3), (1, 4)), ((1, 2), (1, 3)))
    gather_steps(((0, 5), (0, 6)), ())
    from_sibling(0)
    table_copy.wait()
    block_copy.wait()
    multiply(0, 0, 15)
    gather_steps(((2, 4), (1, 5)), ((2, 2),))
    multiply(0, 15, 25)
    rs_first(0)
    contract(0)
    ar(0, 0)
    gather_steps(((1, 6),), ())
    from_sibling(1)
    ar(0, 1)
    gather_steps((), ((2, 3),))
    multiply(1, 0, 15)
    gather_steps(((2, 5),), ())
    multiply(1, 15, 25)
    gather_steps(((2, 6),), ())
    rs_first(1)
    contract(1)
    ar(1, 0)
    rs_second(0)
    ar(0, 2)
    ar(1, 1)
    from_sibling(2)
    multiply(2, 0, 25)
    rs_first(2)
    contract(2)
    ar(2, 0)
    ar(0, 3)
    ar(2, 1)
    rs_second(1)
    ar(1, 2)
    panel(0)
    rs_second(2)
    ar(2, 2)
    ar(1, 3)
    ar(0, 4)
    panel(1)
    ar(2, 3)
    ar(0, 5)
    diag_copy.wait()
    y00 = diag[0] - f0[2]
    y10 = -(f0[0].T + times(y00, new[1, 0]))
    super_out[0] = y00
    super_out[1] = y10
    y20 = -(f0[1].T + (times(y00, new[2, 0]) + times(y10, new[2, 1])))
    super_out[3] = y20
    super_out[2] = diag[1] - times(y10, new[1, 0], True)
    super_out[4] = times(y10.T, new[2, 0])
    super_out[5] = diag[2] - times(y20, new[2, 0], True)
    def send_done(t, n):
        pltpu.make_async_remote_copy(
            lo[t].at[0], lo[t].at[0], lo_send.at[t, n], lo_recv.at[t, 0],
            device_id=sib, device_id_type=MESH,
        ).wait_send()

    @pl.when(is_src & (k == src_k))
    def _():
        for t in range(3):
            for s in range(2):
                send_done(t, 30 + s)

    @pl.when(is_src)
    def _():
        for t, n in sent["src"]:
            send_done(t, n)

    @pl.when(jnp.logical_not(is_src))
    def _():
        for t, n in sent["mid"]:
            send_done(t, n)

    ar(1, 4)
    ar(2, 4)
    panel(2)
    ar(1, 5)
    y11 = super_out[2] - f1[1]
    super_out[2] = y11
    y21 = -(f1[0].T + (super_out[4] + times(y11, new[2, 1])))
    super_out[4] = y21
    rest = super_out[5] - times(y21, new[2, 1], True)
    for t in range(3):
        for n in range(6):
            rs_copy(t, n).wait_send()
    ar(2, 5)
    super_out[5] = rest - f2[0]


def place_kernel(found, out):
    for i in range(3):
        for j in range(3):
            out[i, j] = found[i * (i + 1) // 2 + j] if j <= i else jnp.zeros((256, 256), F32)


def per_device(
    inverse_blocks,
    inverse_rows,
    inverse_cols,
    inverse_count,
    panel_rows,
    lower_old,
    lower_new,
    diag_inverse,
):
    vmem = pl.BlockSpec(memory_space=pltpu.VMEM)
    hbm = pl.BlockSpec(memory_space=pltpu.HBM)

    def each(*shape):
        return [pltpu.VMEM(tuple(nb if s is None else s for s in shape), F32) for nb in BUNDLES]

    panels, found = pl.pallas_call(
        kernel,
        out_shape=(
            jax.ShapeDtypeStruct((3, 2, 64, 256), BF16),
            jax.ShapeDtypeStruct((6, 256, 256), F32),
        ),
        in_specs=[hbm] * 8,
        out_specs=(vmem, vmem),
        scratch_shapes=[
            pltpu.VMEM((1, 96), jnp.int32),
            pltpu.VMEM((1, 96), jnp.int32),
            pltpu.SMEM((1, 1), jnp.int32),
            pltpu.SMEM((64,), jnp.int32),
            pltpu.VMEM((3, 2, 256, 256), BF16),
            pltpu.VMEM((3, 128), jnp.int32),
            pltpu.SMEM((3, 128), jnp.int32),
            pltpu.VMEM((97, 256, 256), BF16),
            *[pltpu.VMEM((16, 256, 256), BF16)] * 3,
            *[pltpu.VMEM((2, 256, 256), F32)] * 3,
            pltpu.VMEM((3, 3, 256, 256), BF16),
            pltpu.VMEM((3, 256, 256), F32),
            pltpu.VMEM((3, 64, 256), F32),
            pltpu.VMEM((3, 64, 256), F32),
            pltpu.VMEM((3, 2, 64, 256), F32),
            pltpu.VMEM((3, 2, 64, 256), F32),
            pltpu.VMEM((3, 128, 256), BF16),
            pltpu.VMEM((3, 256, 512), BF16),
            pltpu.VMEM((3, 512, 256), BF16),
            pltpu.VMEM((3, 512, 256), BF16),
            *each(None, 256, 256),
            *each(None, 128, 256),
            *each(None, 128, 256),
            *each(16, None, 8, 256),
            *each(None, 8, 256),
            *each(4, None, 8, 256),
            *each(None, 256, 256),
            pltpu.SemaphoreType.DMA((9,)),
            pltpu.SemaphoreType.DMA((3, 32)),
            pltpu.SemaphoreType.DMA((3, 16)),
            pltpu.SemaphoreType.DMA((3, 6)),
            pltpu.SemaphoreType.DMA((3, 6)),
            pltpu.SemaphoreType.DMA((3, 7)),
            pltpu.SemaphoreType.DMA((3, 7)),
        ],
        compiler_params=pltpu.CompilerParams(
            collective_id=0, has_side_effects=True, vmem_limit_bytes=60 * 2**20
        ),
    )(inverse_rows, inverse_cols, inverse_count, panel_rows, lower_old, inverse_blocks, lower_new, diag_inverse)
    placed = pl.pallas_call(
        place_kernel,
        out_shape=jax.ShapeDtypeStruct((3, 3, 256, 256), F32),
        in_specs=[vmem],
        out_specs=vmem,
    )(found)
    return panels, placed


def solution(mesh):
    placed = (
        P("row", "col", None, None),
        P("row", "col"),
        P("row", "col"),
        P("row", "col"),
        P(),
        P(None, "row", None, None),
        P(),
        P(),
    )
    return jax.shard_map(
        per_device,
        mesh=mesh,
        in_specs=placed,
        out_specs=(P(None, "row", "col", None), P()),
        check_vma=False,
    )
```

```python
import functools

import jax
import jax.numpy as jnp
from jax import lax
from jax.experimental import pallas as pl
from jax.experimental.pallas import tpu as pltpu
from jax.sharding import PartitionSpec as P

MESH = pl.DeviceIdType.MESH
F32 = jnp.float32
BF16 = jnp.bfloat16
GROUP = 4
BUNDLES = (3, 2, 1)
KINDS = (BF16, BF16, BF16)
PLANE = tuple((dx, dy) for dy in (1, 3, 0, 2) for dx in (1, 3, 0, 2) if (dx, dy) != (0, 0))


def slot_lists(rows, cols, count, panel_rows, row, col):
    kmax = rows.shape[1]
    slot = lax.broadcasted_iota(jnp.int32, (kmax, kmax), 0)
    other = lax.broadcasted_iota(jnp.int32, (kmax, kmax), 1)

    def upright(line):
        return jnp.sum(jnp.where(slot == other, jnp.broadcast_to(line, (kmax, kmax)), 0), axis=1, keepdims=True)

    stored_row, stored_col = upright(rows), upright(cols)
    index = lax.broadcasted_iota(jnp.int32, (kmax, 1), 0)
    live = index < count
    useful = jnp.zeros((kmax, 1), jnp.int32)
    position = jnp.zeros((kmax, 1), jnp.int32)
    for i in range(8):
        for j in range(2):
            same = stored_col == panel_rows[(i * 4 + col) * 2 + j]
            useful = jnp.where(same & live, 1, useful)
            position = jnp.where(same, i * 2 + j, position)
    mine = [jnp.where(stored_row == panel_rows[row * 2 + p], useful, 0) for p in range(2)]
    flat = [jnp.sum(jnp.where(slot == other, jnp.broadcast_to(m, (kmax, kmax)), 0), axis=0, keepdims=True) for m in mine]
    rank = [
        jnp.sum(jnp.where(other < slot, jnp.broadcast_to(f, (kmax, kmax)), 0), axis=1, keepdims=True) for f in flat
    ]
    first = jnp.sum(jnp.broadcast_to(flat[0], (8, kmax)), axis=1, keepdims=True)[0:1]
    padding = jnp.where(first % GROUP == 0, 0, GROUP - first % GROUP)
    start = first + padding
    place = jnp.where(mine[0] == 1, rank[0], jnp.where(mine[1] == 1, start + rank[1], -1))
    hit = place == lax.broadcasted_iota(jnp.int32, (kmax, 128), 1)
    filled = jnp.sum(jnp.where(hit, 1, 0), axis=0, keepdims=True)
    slot_at = jnp.sum(jnp.where(hit, index, 0), axis=0, keepdims=True)
    cand_at = jnp.sum(jnp.where(hit, position, 0), axis=0, keepdims=True)
    lane = lax.broadcasted_iota(jnp.int32, (1, 128), 1)
    is_first = jnp.where(lane * GROUP < start, 1, 0)
    return jnp.where(filled == 1, slot_at, kmax), cand_at, is_first


def kernel(
    rows_hbm, cols_hbm, count_hbm, panel_hbm, low_hbm, blocks_hbm, new_hbm, diag_hbm,
    panel_out, super_out,
    rows, cols, count, panel_rows, low, lists, table,
    blocks, lo0, lo1, lo2, acc0, acc1, acc2, new, diag,
    rs_a, rs_b, rs_p, rs_m, u_all, low_t, v_high, v_low,
    g0, g1, g2, c0, c1, c2, h0, h1, h2, p0, p1, p2, s0, s1, s2, y0, y1, y2, f0, f1, f2,
    local_sem, lo_send, lo_recv, rs_send, rs_recv, ar_send, ar_recv,
):
    lo = (lo0, lo1, lo2)
    acc = (acc0, acc1, acc2)
    row = lax.axis_index("row")
    z = lax.axis_index("col")
    y = row // 8
    x = (row // 2) % 4
    k = row % 2
    sib = (y * 8 + x * 2 + (1 - k), z)

    def at(dx=0, dy=0, dz=0):
        return ((y + dy + 4) % 4 * 8 + (x + dx + 4) % 4 * 2 + k, (z + dz + 4) % 4)

    barrier = pltpu.get_barrier_semaphore()
    partners = [sib]
    partners += [at(dx=dx, dy=dy) for dx, dy in PLANE]
    partners += [at(dz=d) for d in (1, 2, 3)]
    for dev in partners:
        pl.semaphore_signal(barrier, inc=1, device_id=dev, device_id_type=MESH)

    block_copy = pltpu.make_async_copy(blocks_hbm.at[0], blocks.at[pl.ds(0, 96)], local_sem.at[0])
    new_copy = pltpu.make_async_copy(new_hbm, new, local_sem.at[1])
    diag_copy = pltpu.make_async_copy(diag_hbm, diag, local_sem.at[2])
    low_copy = pltpu.make_async_copy(low_hbm, low, local_sem.at[4])
    index_copies = [
        pltpu.make_async_copy(src, dst, local_sem.at[5 + i])
        for i, (src, dst) in enumerate(
            ((rows_hbm, rows), (cols_hbm, cols), (count_hbm, count), (panel_hbm, panel_rows))
        )
    ]
    low_copy.start()
    for c in index_copies:
        c.start()
    block_copy.start()
    new_copy.start()
    diag_copy.start()
    blocks[96] = jnp.zeros((256, 256), BF16)

    src_x = z // 2
    src_k = z % 2
    is_src = x % 2 == src_x
    def piece(half, yy, slot):
        return ((yy + 8) % 4 * 2 + half) * 2 + slot

    own_half = x // 2
    left_half = (x + 3) % 4 // 2
    right_half = (x + 1) % 4 // 2
    far_half = 1 - own_half

    sent = {"src": [], "mid": []}

    def send(role, t, cand, dev):
        n = len([1 for (tt, _) in sent[role] if tt == t])
        sent[role].append((t, n))
        pltpu.make_async_remote_copy(
            lo[t].at[cand], lo[t].at[cand], lo_send.at[t, n], lo_recv.at[t, cand],
            device_id=dev, device_id_type=MESH,
        ).start()

    def arrived(t, cand):
        pltpu.make_async_remote_copy(
            lo[t].at[cand], lo[t].at[cand], lo_send.at[t, 0], lo_recv.at[t, cand],
            device_id=sib, device_id_type=MESH,
        ).wait_recv()

    def src_step(t, step):
        if step == 1:
            own = piece(own_half, y, k)
            for dev in (at(dx=1), at(dx=-1), at(dy=1), at(dy=-1), at(dy=2)):
                send("src", t, own, dev)
        if step == 2:
            for d in (1, 3):
                c = piece(own_half, y + d, k)
                arrived(t, c)
                send("src", t, c, sib)
        if step == 3:
            c = piece(own_half, y + 2, k)
            arrived(t, c)
            send("src", t, c, at(dx=1))
            send("src", t, c, at(dx=-1))
            send("src", t, c, sib)
        if step >= 4:
            for d in {4: (0,), 5: (1, 3), 6: (2,)}[step]:
                c = piece(far_half, y + d, k)
                arrived(t, c)
                send("src", t, c, sib)

    def mid_step(t, step):
        for d in {1: (0,), 2: (3, 1), 3: (2,)}[step]:
            c = piece(left_half, y + d, k)
            arrived(t, c)
            if d == 0:
                send("mid", t, c, at(dy=1))
                send("mid", t, c, at(dy=-1))
            if d in (0, 1):
                send("mid", t, c, at(dx=1))
            send("mid", t, c, sib)
            c = piece(right_half, y + d, k)
            arrived(t, c)
            if d == 0:
                send("mid", t, c, at(dy=1))
                send("mid", t, c, at(dy=-1))
            if d in (2, 3):
                send("mid", t, c, at(dx=-1))
            send("mid", t, c, sib)

    def gather_steps(src_steps, mid_steps):
        @pl.when(is_src)
        def _():
            for t, step in src_steps:
                src_step(t, step)

        @pl.when(jnp.logical_not(is_src))
        def _():
            for t, step in mid_steps:
                mid_step(t, step)

    def from_sibling(t):
        @pl.when(is_src)
        def _():
            for d in (1, 2, 3):
                arrived(t, piece(own_half, y + d, 1 - k))
            for d in range(4):
                arrived(t, piece(far_half, y + d, 1 - k))

        @pl.when(jnp.logical_not(is_src))
        def _():
            for d in range(4):
                arrived(t, piece(left_half, y + d, 1 - k))
                arrived(t, piece(right_half, y + d, 1 - k))

    def multiply(t, begin, end):
        if begin == 0:
            acc[t][...] = jnp.zeros((2, 256, 256), F32)

        def body(g, carry):
            left = [blocks[table[0, g * GROUP + i]] for i in range(GROUP)]
            right = [lo[t][table[1, g * GROUP + i]] for i in range(GROUP)]
            product = jnp.dot(
                jnp.concatenate(left, axis=1), jnp.concatenate(right, axis=0), preferred_element_type=F32
            )
            weight = table[2, g].astype(F32)
            acc[t][0] += product * weight
            acc[t][1] += product * (1.0 - weight)
            return carry

        lax.fori_loop(begin, end, body, 0, unroll=5)

    def quarter(d):
        return pl.ds(pl.multiple_of((z + d) % 4 * 64, 64), 64)

    def rs_copy(t, n):
        a = acc[t]
        src, dst, dev = (
            (a.at[0, quarter(2)], rs_a.at[t], at(dz=1)),
            (a.at[1, quarter(2)], rs_b.at[t], at(dz=3)),
            (a.at[1, quarter(1)], rs_p.at[t, 1], at(dz=1)),
            (a.at[0, quarter(3)], rs_m.at[t, 0], at(dz=3)),
            (a.at[0, quarter(1)], rs_p.at[t, 0], at(dz=1)),
            (a.at[1, quarter(3)], rs_m.at[t, 1], at(dz=3)),
        )[n]
        return pltpu.make_async_remote_copy(
            src, dst, rs_send.at[t, n], rs_recv.at[t, n], device_id=dev, device_id_type=MESH
        )

    def rs_first(t):
        for n in range(4):
            rs_copy(t, n).start()

    def rs_second(t):
        rs_copy(t, 0).wait_recv()
        acc[t][0, quarter(1)] += rs_a[t]
        rs_copy(t, 4).start()
        rs_copy(t, 1).wait_recv()
        acc[t][1, quarter(3)] += rs_b[t]
        rs_copy(t, 5).start()

    def rs_third(t):
        for n in (2, 3, 4, 5):
            rs_copy(t, n).wait_recv()
        return (acc[t][:, quarter(0)] + (rs_p[t] + rs_m[t])).reshape(128, 256)

    def across(left, right):
        return lax.dot_general(left, right, (((0,), (0,)), ((), ())), preferred_element_type=F32)

    g = (g0, g1, g2)

    def panel(t):
        running = rs_third(t)
        for e in range(t):
            running = running + jnp.dot(u_all[e], new[t, e], preferred_element_type=F32)
        current = (-running).astype(BF16)
        u_all[t] = current
        panel_out[t] = current.reshape(2, 64, 256)

    def halves(value):
        high = value.astype(BF16)
        return high, (value - high.astype(F32)).astype(BF16)

    def turn_low():
        for t in range(3):
            low_t[t] = low[t].reshape(512, 256).T

    def contract(t):
        for p in range(2):
            rows_p = pl.ds(256 * p, 256)
            value = acc[t][p]
            for e in range(t):
                for part in (v_low, v_high):
                    value = value + jnp.dot(part[e, rows_p], new[t, e], preferred_element_type=F32)
            v_high[t, rows_p], v_low[t, rows_p] = halves(-value)
        for i, other in enumerate({0: (1, 2, 0), 1: (2, 1), 2: (2,)}[t]):
            g[t][i] = jnp.dot(low_t[other], v_low[t], preferred_element_type=F32) + jnp.dot(
                low_t[other], v_high[t], preferred_element_type=F32
            )

    def ar(b, phase):
        gb, cb, hb, pb, sb, yb, fb = (
            (g0, c0, h0, p0, s0, y0, f0),
            (g1, c1, h1, p1, s1, y1, f1),
            (g2, c2, h2, p2, s2, y2, f2),
        )[b]

        def ds(start, size):
            return pl.ds(pl.multiple_of(start, size), size)

        def copy(n, src, dst, dev):
            return pltpu.make_async_remote_copy(
                src, dst, ar_send.at[b, n], ar_recv.at[b, n], device_id=dev, device_id_type=MESH
            )

        mine = y * 4 + x
        base = 16 * k + mine
        peers = [(dx, dy) for dx, dy in PLANE]

        def core():
            return [copy(0, gb.at[:, ds(128 * (1 - k), 128)], cb, sib)]

        def over_plane():
            copies = []
            for dx, dy in peers:
                other = (y + dy) % 4 * 4 + (x + dx) % 4
                copies.append(copy(1, hb.at[:, other], pb.at[mine], at(dx=dx, dy=dy)))
            return copies

        def over_z():
            return [copy(1 + d, sb, yb.at[z], at(dz=d)) for d in (1, 3, 2)]

        def back_plane():
            part = fb.at[:, base]
            return [copy(5, part, part, at(dx=dx, dy=dy)) for dx, dy in peers]

        def back_core():
            part = fb.at[:, ds(16 * k, 16)]
            return [copy(6, part, part, sib)]

        def plane_wait():
            return [copy(1, hb.at[:, pl.ds(0, 15)], hb.at[:, pl.ds(0, 15)], sib)]

        def back_wait():
            return [copy(5, fb.at[:, pl.ds(0, 15)], fb.at[:, pl.ds(0, 15)], sib)]

        stages = (core, over_plane, over_z, back_plane, back_core)
        waits = (core, plane_wait, over_z, back_wait, back_core)
        if phase > 0:
            for c in waits[phase - 1]():
                c.wait_recv()
        if phase == 1:
            half = gb[:, ds(128 * k, 128)] + cb[...]
            hb[...] = half.reshape(hb.shape).astype(hb.dtype)
            pb[mine] = hb[:, mine]
        if phase == 2:
            total = [pb[i].astype(F32) for i in range(16)]
            while len(total) > 1:
                total = [total[i] + total[i + 1] for i in range(0, len(total), 2)]
            sb[...] = total[0]
            yb[z] = total[0]
        if phase == 3:
            fb[:, base] = ((yb[0] + yb[1]) + (yb[2] + yb[3])).astype(fb.dtype)
        if phase < 5:
            for c in stages[phase]():
                c.start()
        if phase == 5:
            for stage in waits:
                for c in stage():
                    c.wait_send()

    def times(value, factor, turned=False):
        total = None
        for part in halves(value):
            if turned:
                term = across(factor, part)
            else:
                term = jnp.dot(part, factor, preferred_element_type=F32)
            total = term if total is None else total + term
        return total

    def summed(f, i):
        return f[i].reshape(256, 256).astype(F32)

    low_copy.wait()
    pl.semaphore_wait(barrier, len(partners))

    @pl.when(is_src & (k == src_k))
    def _():
        own = piece(own_half, y, 0)
        for t in range(3):
            for s in range(2):
                lo[t][own + s] = low[t, s]
                pltpu.make_async_remote_copy(
                    lo[t].at[own + s], lo[t].at[own + s], lo_send.at[t, 30 + s], lo_recv.at[t, own + s],
                    device_id=sib, device_id_type=MESH,
                ).start()

    @pl.when(is_src & (k != src_k))
    def _():
        own = piece(own_half, y, 0)
        for t in range(3):
            for s in range(2):
                arrived(t, own + s)

    gather_steps(((0, 1), (1, 1), (2, 1)), ())
    for c in index_copies:
        c.wait()
    found = slot_lists(rows[...], cols[...], count[0, 0], panel_rows, row, z)
    for i in range(3):
        lists[i : i + 1, :] = found[i]
    table_copy = pltpu.make_async_copy(lists, table, local_sem.at[3])
    table_copy.start()
    turn_low()
    new_copy.wait()
    gather_steps(((0, 2),), ((0, 1),))
    gather_steps(((1, 2), (0, 3)), ((1, 1),))
    gather_steps(((2, 2), (1, 3), (0, 4)), ((2, 1), (0, 2), (0, 3)))
    gather_steps(((2, 3), (1, 4)), ((1, 2), (1, 3)))
    gather_steps(((0, 5), (0, 6)), ())
    from_sibling(0)
    table_copy.wait()
    block_copy.wait()
    multiply(0, 0, 15)
    gather_steps(((2, 4), (1, 5)), ((2, 2),))
    multiply(0, 15, 25)
    rs_first(0)
    contract(0)
    ar(0, 0)
    gather_steps(((1, 6),), ())
    from_sibling(1)
    ar(0, 1)
    gather_steps((), ((2, 3),))
    multiply(1, 0, 15)
    gather_steps(((2, 5),), ())
    multiply(1, 15, 25)
    gather_steps(((2, 6),), ())
    rs_first(1)
    contract(1)
    ar(1, 0)
    rs_second(0)
    ar(0, 2)
    ar(1, 1)
    from_sibling(2)
    multiply(2, 0, 25)
    rs_first(2)
    contract(2)
    ar(2, 0)
    ar(0, 3)
    ar(2, 1)
    rs_second(1)
    ar(1, 2)
    panel(0)
    rs_second(2)
    ar(2, 2)
    ar(1, 3)
    ar(0, 4)
    panel(1)
    ar(2, 3)
    ar(0, 5)
    diag_copy.wait()
    y00 = diag[0] - summed(f0, 2)
    y10 = -(summed(f0, 0).T + times(y00, new[1, 0]))
    super_out[0] = y00
    super_out[1] = y10
    y20 = -(summed(f0, 1).T + (times(y00, new[2, 0]) + times(y10, new[2, 1])))
    super_out[3] = y20
    super_out[2] = diag[1] - times(y10, new[1, 0], True)
    super_out[4] = times(y10.T, new[2, 0])
    super_out[5] = diag[2] - times(y20, new[2, 0], True)
    def send_done(t, n):
        pltpu.make_async_remote_copy(
            lo[t].at[0], lo[t].at[0], lo_send.at[t, n], lo_recv.at[t, 0],
            device_id=sib, device_id_type=MESH,
        ).wait_send()

    @pl.when(is_src & (k == src_k))
    def _():
        for t in range(3):
            for s in range(2):
                send_done(t, 30 + s)

    @pl.when(is_src)
    def _():
        for t, n in sent["src"]:
            send_done(t, n)

    @pl.when(jnp.logical_not(is_src))
    def _():
        for t, n in sent["mid"]:
            send_done(t, n)

    ar(1, 4)
    ar(2, 4)
    panel(2)
    ar(1, 5)
    y11 = super_out[2] - summed(f1, 1)
    super_out[2] = y11
    y21 = -(summed(f1, 0).T + (super_out[4] + times(y11, new[2, 1])))
    super_out[4] = y21
    rest = super_out[5] - times(y21, new[2, 1], True)
    for t in range(3):
        for n in range(6):
            rs_copy(t, n).wait_send()
    ar(2, 5)
    super_out[5] = rest - summed(f2, 0)


def place_kernel(found, out):
    for i in range(3):
        for j in range(3):
            out[i, j] = found[i * (i + 1) // 2 + j] if j <= i else jnp.zeros((256, 256), F32)


def per_device(
    inverse_blocks,
    inverse_rows,
    inverse_cols,
    inverse_count,
    panel_rows,
    lower_old,
    lower_new,
    diag_inverse,
):
    vmem = pl.BlockSpec(memory_space=pltpu.VMEM)
    hbm = pl.BlockSpec(memory_space=pltpu.HBM)

    def sent(*shape):
        return [
            pltpu.VMEM(tuple(nb if s is None else s for s in shape), kind) for nb, kind in zip(BUNDLES, KINDS)
        ]

    def each(*shape):
        return [pltpu.VMEM(tuple(nb if s is None else s for s in shape), F32) for nb in BUNDLES]

    panels, found = pl.pallas_call(
        kernel,
        out_shape=(
            jax.ShapeDtypeStruct((3, 2, 64, 256), BF16),
            jax.ShapeDtypeStruct((6, 256, 256), F32),
        ),
        in_specs=[hbm] * 8,
        out_specs=(vmem, vmem),
        scratch_shapes=[
            pltpu.VMEM((1, 96), jnp.int32),
            pltpu.VMEM((1, 96), jnp.int32),
            pltpu.SMEM((1, 1), jnp.int32),
            pltpu.SMEM((64,), jnp.int32),
            pltpu.VMEM((3, 2, 256, 256), BF16),
            pltpu.VMEM((3, 128), jnp.int32),
            pltpu.SMEM((3, 128), jnp.int32),
            pltpu.VMEM((97, 256, 256), BF16),
            *[pltpu.VMEM((16, 256, 256), BF16)] * 3,
            *[pltpu.VMEM((2, 256, 256), F32)] * 3,
            pltpu.VMEM((3, 3, 256, 256), BF16),
            pltpu.VMEM((3, 256, 256), F32),
            pltpu.VMEM((3, 64, 256), F32),
            pltpu.VMEM((3, 64, 256), F32),
            pltpu.VMEM((3, 2, 64, 256), F32),
            pltpu.VMEM((3, 2, 64, 256), F32),
            pltpu.VMEM((3, 128, 256), BF16),
            pltpu.VMEM((3, 256, 512), BF16),
            pltpu.VMEM((3, 512, 256), BF16),
            pltpu.VMEM((3, 512, 256), BF16),
            *each(None, 256, 256),
            *each(None, 128, 256),
            *sent(None, 16, 8, 256),
            *sent(16, None, 8, 256),
            *each(None, 8, 256),
            *each(4, None, 8, 256),
            *sent(None, 32, 8, 256),
            pltpu.SemaphoreType.DMA((9,)),
            pltpu.SemaphoreType.DMA((3, 32)),
            pltpu.SemaphoreType.DMA((3, 16)),
            pltpu.SemaphoreType.DMA((3, 6)),
            pltpu.SemaphoreType.DMA((3, 6)),
            pltpu.SemaphoreType.DMA((3, 7)),
            pltpu.SemaphoreType.DMA((3, 7)),
        ],
        compiler_params=pltpu.CompilerParams(
            collective_id=0, has_side_effects=True, vmem_limit_bytes=60 * 2**20
        ),
    )(inverse_rows, inverse_cols, inverse_count, panel_rows, lower_old, inverse_blocks, lower_new, diag_inverse)
    placed = pl.pallas_call(
        place_kernel,
        out_shape=jax.ShapeDtypeStruct((3, 3, 256, 256), F32),
        in_specs=[vmem],
        out_specs=vmem,
    )(found)
    return panels, placed


def solution(mesh):
    placed = (
        P("row", "col", None, None),
        P("row", "col"),
        P("row", "col"),
        P("row", "col"),
        P(),
        P(None, "row", None, None),
        P(),
        P(),
    )
    return jax.shard_map(
        per_device,
        mesh=mesh,
        in_specs=placed,
        out_specs=(P(None, "row", "col", None), P()),
        check_vma=False,
    )
```

```python
import functools

import jax
import jax.numpy as jnp
from jax import lax
from jax.experimental import pallas as pl
from jax.experimental.pallas import tpu as pltpu
from jax.sharding import PartitionSpec as P

MESH = pl.DeviceIdType.MESH
F32 = jnp.float32
BF16 = jnp.bfloat16
GROUP = 4
BUNDLES = (3, 2, 1)
KINDS = (BF16, BF16, BF16)
PLANE = tuple((dx, dy) for dy in (1, 3, 0, 2) for dx in (1, 3, 0, 2) if (dx, dy) != (0, 0))


def slot_lists(rows, cols, count, panel_rows, row, col):
    kmax = rows.shape[1]
    slot = lax.broadcasted_iota(jnp.int32, (kmax, kmax), 0)
    other = lax.broadcasted_iota(jnp.int32, (kmax, kmax), 1)

    def upright(line):
        return jnp.sum(jnp.where(slot == other, jnp.broadcast_to(line, (kmax, kmax)), 0), axis=1, keepdims=True)

    stored_row, stored_col = upright(rows), upright(cols)
    index = lax.broadcasted_iota(jnp.int32, (kmax, 1), 0)
    live = index < count
    useful = jnp.zeros((kmax, 1), jnp.int32)
    position = jnp.zeros((kmax, 1), jnp.int32)
    for i in range(8):
        for j in range(2):
            same = stored_col == panel_rows[(i * 4 + col) * 2 + j]
            useful = jnp.where(same & live, 1, useful)
            position = jnp.where(same, i * 2 + j, position)
    mine = [jnp.where(stored_row == panel_rows[row * 2 + p], useful, 0) for p in range(2)]
    flat = [jnp.sum(jnp.where(slot == other, jnp.broadcast_to(m, (kmax, kmax)), 0), axis=0, keepdims=True) for m in mine]
    rank = [
        jnp.sum(jnp.where(other < slot, jnp.broadcast_to(f, (kmax, kmax)), 0), axis=1, keepdims=True) for f in flat
    ]
    first = jnp.sum(jnp.broadcast_to(flat[0], (8, kmax)), axis=1, keepdims=True)[0:1]
    padding = jnp.where(first % GROUP == 0, 0, GROUP - first % GROUP)
    start = first + padding
    place = jnp.where(mine[0] == 1, rank[0], jnp.where(mine[1] == 1, start + rank[1], -1))
    hit = place == lax.broadcasted_iota(jnp.int32, (kmax, 128), 1)
    filled = jnp.sum(jnp.where(hit, 1, 0), axis=0, keepdims=True)
    slot_at = jnp.sum(jnp.where(hit, index, 0), axis=0, keepdims=True)
    cand_at = jnp.sum(jnp.where(hit, position, 0), axis=0, keepdims=True)
    lane = lax.broadcasted_iota(jnp.int32, (1, 128), 1)
    is_first = jnp.where(lane * GROUP < start, 1, 0)
    return jnp.where(filled == 1, slot_at, kmax), cand_at, is_first


def kernel(
    rows_hbm, cols_hbm, count_hbm, panel_hbm, low_hbm, blocks_hbm, new_hbm, diag_hbm,
    panel_out, super_out,
    rows, cols, count, panel_rows, low, lists, table,
    blocks, lo0, lo1, lo2, acc0, acc1, acc2, new, diag,
    rs_a, rs_b, rs_p, rs_m, u_all, low_t, v_high, v_low,
    g0, g1, g2, c0, c1, c2, h0, h1, h2, p0, p1, p2, s0, s1, s2, y0, y1, y2, f0, f1, f2,
    local_sem, lo_send, lo_recv, rs_send, rs_recv, ar_send, ar_recv,
):
    lo = (lo0, lo1, lo2)
    acc = (acc0, acc1, acc2)
    row = lax.axis_index("row")
    z = lax.axis_index("col")
    y = row // 8
    x = (row // 2) % 4
    k = row % 2
    sib = (y * 8 + x * 2 + (1 - k), z)

    def at(dx=0, dy=0, dz=0):
        return ((y + dy + 4) % 4 * 8 + (x + dx + 4) % 4 * 2 + k, (z + dz + 4) % 4)

    barrier = pltpu.get_barrier_semaphore()
    partners = [sib]
    partners += [at(dx=dx, dy=dy) for dx, dy in PLANE]
    partners += [at(dz=d) for d in (1, 2, 3)]
    for dev in partners:
        pl.semaphore_signal(barrier, inc=1, device_id=dev, device_id_type=MESH)

    block_copy = pltpu.make_async_copy(blocks_hbm.at[0], blocks.at[pl.ds(0, 96)], local_sem.at[0])
    new_copy = pltpu.make_async_copy(new_hbm, new, local_sem.at[1])
    diag_copy = pltpu.make_async_copy(diag_hbm, diag, local_sem.at[2])
    low_copy = pltpu.make_async_copy(low_hbm, low, local_sem.at[4])
    index_copies = [
        pltpu.make_async_copy(src, dst, local_sem.at[5 + i])
        for i, (src, dst) in enumerate(
            ((rows_hbm, rows), (cols_hbm, cols), (count_hbm, count), (panel_hbm, panel_rows))
        )
    ]
    low_copy.start()
    for c in index_copies:
        c.start()
    block_copy.start()
    new_copy.start()
    diag_copy.start()
    blocks[96] = jnp.zeros((256, 256), BF16)

    src_x = z // 2
    src_k = z % 2
    is_src = x % 2 == src_x
    def piece(half, yy, slot):
        return ((yy + 8) % 4 * 2 + half) * 2 + slot

    own_half = x // 2
    left_half = (x + 3) % 4 // 2
    right_half = (x + 1) % 4 // 2
    far_half = 1 - own_half

    sent = {"src": [], "mid": []}

    def send(role, t, cand, dev):
        n = len([1 for (tt, _) in sent[role] if tt == t])
        sent[role].append((t, n))
        pltpu.make_async_remote_copy(
            lo[t].at[cand], lo[t].at[cand], lo_send.at[t, n], lo_recv.at[t, cand],
            device_id=dev, device_id_type=MESH,
        ).start()

    def arrived(t, cand):
        pltpu.make_async_remote_copy(
            lo[t].at[cand], lo[t].at[cand], lo_send.at[t, 0], lo_recv.at[t, cand],
            device_id=sib, device_id_type=MESH,
        ).wait_recv()

    def src_step(t, step):
        if step == 1:
            own = piece(own_half, y, k)
            for dev in (at(dx=1), at(dx=-1), at(dy=1), at(dy=-1), at(dy=2)):
                send("src", t, own, dev)
        if step == 2:
            for d in (1, 3):
                c = piece(own_half, y + d, k)
                arrived(t, c)
                send("src", t, c, sib)
        if step == 3:
            c = piece(own_half, y + 2, k)
            arrived(t, c)
            send("src", t, c, at(dx=1))
            send("src", t, c, at(dx=-1))
            send("src", t, c, sib)
        if step >= 4:
            for d in {4: (0,), 5: (1, 3), 6: (2,)}[step]:
                c = piece(far_half, y + d, k)
                arrived(t, c)
                send("src", t, c, sib)

    def mid_step(t, step):
        for d in {1: (0,), 2: (3, 1), 3: (2,)}[step]:
            c = piece(left_half, y + d, k)
            arrived(t, c)
            if d == 0:
                send("mid", t, c, at(dy=1))
                send("mid", t, c, at(dy=-1))
            if d in (0, 1):
                send("mid", t, c, at(dx=1))
            send("mid", t, c, sib)
            c = piece(right_half, y + d, k)
            arrived(t, c)
            if d == 0:
                send("mid", t, c, at(dy=1))
                send("mid", t, c, at(dy=-1))
            if d in (2, 3):
                send("mid", t, c, at(dx=-1))
            send("mid", t, c, sib)

    def gather_steps(src_steps, mid_steps):
        @pl.when(is_src)
        def _():
            for t, step in src_steps:
                src_step(t, step)

        @pl.when(jnp.logical_not(is_src))
        def _():
            for t, step in mid_steps:
                mid_step(t, step)

    def from_sibling(t):
        @pl.when(is_src)
        def _():
            for d in (1, 2, 3):
                arrived(t, piece(own_half, y + d, 1 - k))
            for d in range(4):
                arrived(t, piece(far_half, y + d, 1 - k))

        @pl.when(jnp.logical_not(is_src))
        def _():
            for d in range(4):
                arrived(t, piece(left_half, y + d, 1 - k))
                arrived(t, piece(right_half, y + d, 1 - k))

    def multiply(t, begin, end):
        if begin == 0:
            acc[t][...] = jnp.zeros((2, 256, 256), F32)

        def body(g, carry):
            left = [blocks[table[0, g * GROUP + i]] for i in range(GROUP)]
            right = [lo[t][table[1, g * GROUP + i]] for i in range(GROUP)]
            product = jnp.dot(
                jnp.concatenate(left, axis=1), jnp.concatenate(right, axis=0), preferred_element_type=F32
            )
            weight = table[2, g].astype(F32)
            acc[t][0] += product * weight
            acc[t][1] += product * (1.0 - weight)
            return carry

        lax.fori_loop(begin, end, body, 0, unroll=25 if t == 2 else 5)

    def quarter(d):
        return pl.ds(pl.multiple_of((z + d) % 4 * 64, 64), 64)

    def rs_copy(t, n):
        a = acc[t]
        src, dst, dev = (
            (a.at[0, quarter(2)], rs_a.at[t], at(dz=1)),
            (a.at[1, quarter(2)], rs_b.at[t], at(dz=3)),
            (a.at[1, quarter(1)], rs_p.at[t, 1], at(dz=1)),
            (a.at[0, quarter(3)], rs_m.at[t, 0], at(dz=3)),
            (a.at[0, quarter(1)], rs_p.at[t, 0], at(dz=1)),
            (a.at[1, quarter(3)], rs_m.at[t, 1], at(dz=3)),
        )[n]
        return pltpu.make_async_remote_copy(
            src, dst, rs_send.at[t, n], rs_recv.at[t, n], device_id=dev, device_id_type=MESH
        )

    def rs_first(t):
        for n in range(4):
            rs_copy(t, n).start()

    def rs_second(t):
        rs_copy(t, 0).wait_recv()
        acc[t][0, quarter(1)] += rs_a[t]
        rs_copy(t, 4).start()
        rs_copy(t, 1).wait_recv()
        acc[t][1, quarter(3)] += rs_b[t]
        rs_copy(t, 5).start()

    def rs_third(t):
        for n in (2, 3, 4, 5):
            rs_copy(t, n).wait_recv()
        return (acc[t][:, quarter(0)] + (rs_p[t] + rs_m[t])).reshape(128, 256)

    def across(left, right):
        return lax.dot_general(left, right, (((0,), (0,)), ((), ())), preferred_element_type=F32)

    g = (g0, g1, g2)

    def panel(t):
        running = rs_third(t)
        for e in range(t):
            running = running + jnp.dot(u_all[e], new[t, e], preferred_element_type=F32)
        current = (-running).astype(BF16)
        u_all[t] = current
        panel_out[t] = current.reshape(2, 64, 256)

    def halves(value):
        high = value.astype(BF16)
        return high, (value - high.astype(F32)).astype(BF16)

    def turn_low():
        for t in range(3):
            low_t[t] = low[t].reshape(512, 256).T

    def contract(t):
        for p in range(2):
            rows_p = pl.ds(256 * p, 256)
            value = acc[t][p]
            for e in range(t):
                for part in (v_low, v_high):
                    value = value + jnp.dot(part[e, rows_p], new[t, e], preferred_element_type=F32)
            v_high[t, rows_p], v_low[t, rows_p] = halves(-value)
        for i, other in enumerate({0: (1, 2, 0), 1: (2, 1), 2: (2,)}[t]):
            g[t][i] = jnp.dot(low_t[other], v_low[t], preferred_element_type=F32) + jnp.dot(
                low_t[other], v_high[t], preferred_element_type=F32
            )

    def ar(b, phase):
        gb, cb, hb, pb, sb, yb, fb = (
            (g0, c0, h0, p0, s0, y0, f0),
            (g1, c1, h1, p1, s1, y1, f1),
            (g2, c2, h2, p2, s2, y2, f2),
        )[b]

        def ds(start, size):
            return pl.ds(pl.multiple_of(start, size), size)

        def copy(n, src, dst, dev):
            return pltpu.make_async_remote_copy(
                src, dst, ar_send.at[b, n], ar_recv.at[b, n], device_id=dev, device_id_type=MESH
            )

        mine = y * 4 + x
        base = 16 * k + mine
        peers = [(dx, dy) for dx, dy in PLANE]

        def core():
            return [copy(0, gb.at[:, ds(128 * (1 - k), 128)], cb, sib)]

        def over_plane():
            copies = []
            for dx, dy in peers:
                other = (y + dy) % 4 * 4 + (x + dx) % 4
                copies.append(copy(1, hb.at[:, other], pb.at[mine], at(dx=dx, dy=dy)))
            return copies

        def over_z():
            return [copy(1 + d, sb, yb.at[z], at(dz=d)) for d in (1, 3, 2)]

        def back_plane():
            part = fb.at[:, base]
            return [copy(5, part, part, at(dx=dx, dy=dy)) for dx, dy in peers]

        def back_core():
            part = fb.at[:, ds(16 * k, 16)]
            return [copy(6, part, part, sib)]

        def plane_wait():
            return [copy(1, hb.at[:, pl.ds(0, 15)], hb.at[:, pl.ds(0, 15)], sib)]

        def back_wait():
            return [copy(5, fb.at[:, pl.ds(0, 15)], fb.at[:, pl.ds(0, 15)], sib)]

        stages = (core, over_plane, over_z, back_plane, back_core)
        waits = (core, plane_wait, over_z, back_wait, back_core)
        if phase > 0:
            for c in waits[phase - 1]():
                c.wait_recv()
        if phase == 1:
            half = gb[:, ds(128 * k, 128)] + cb[...]
            hb[...] = half.reshape(hb.shape).astype(hb.dtype)
            pb[mine] = hb[:, mine]
        if phase == 2:
            total = [pb[i].astype(F32) for i in range(16)]
            while len(total) > 1:
                total = [total[i] + total[i + 1] for i in range(0, len(total), 2)]
            sb[...] = total[0]
            yb[z] = total[0]
        if phase == 3:
            fb[:, base] = ((yb[0] + yb[1]) + (yb[2] + yb[3])).astype(fb.dtype)
        if phase < 5:
            for c in stages[phase]():
                c.start()
        if phase == 5:
            for stage in waits:
                for c in stage():
                    c.wait_send()

    def times(value, factor, turned=False):
        total = None
        for part in halves(value):
            if turned:
                term = across(factor, part)
            else:
                term = jnp.dot(part, factor, preferred_element_type=F32)
            total = term if total is None else total + term
        return total

    def summed(f, i):
        return f[i].reshape(256, 256).astype(F32)

    low_copy.wait()
    pl.semaphore_wait(barrier, len(partners))

    @pl.when(is_src & (k == src_k))
    def _():
        own = piece(own_half, y, 0)
        for t in range(3):
            for s in range(2):
                lo[t][own + s] = low[t, s]
                pltpu.make_async_remote_copy(
                    lo[t].at[own + s], lo[t].at[own + s], lo_send.at[t, 30 + s], lo_recv.at[t, own + s],
                    device_id=sib, device_id_type=MESH,
                ).start()

    @pl.when(is_src & (k != src_k))
    def _():
        own = piece(own_half, y, 0)
        for t in range(3):
            for s in range(2):
                arrived(t, own + s)

    gather_steps(((0, 1), (1, 1), (2, 1)), ())
    for c in index_copies:
        c.wait()
    found = slot_lists(rows[...], cols[...], count[0, 0], panel_rows, row, z)
    for i in range(3):
        lists[i : i + 1, :] = found[i]
    table_copy = pltpu.make_async_copy(lists, table, local_sem.at[3])
    table_copy.start()
    turn_low()
    new_copy.wait()
    gather_steps(((0, 2),), ((0, 1),))
    gather_steps(((1, 2), (0, 3)), ((1, 1),))
    gather_steps(((2, 2), (1, 3), (0, 4)), ((2, 1), (0, 2), (0, 3)))
    gather_steps(((2, 3), (1, 4)), ((1, 2), (1, 3)))
    gather_steps(((0, 5), (0, 6)), ())
    from_sibling(0)
    table_copy.wait()
    block_copy.wait()
    multiply(0, 0, 15)
    gather_steps(((2, 4), (1, 5)), ((2, 2),))
    multiply(0, 15, 25)
    rs_first(0)
    contract(0)
    ar(0, 0)
    gather_steps(((1, 6),), ())
    from_sibling(1)
    ar(0, 1)
    gather_steps((), ((2, 3),))
    multiply(1, 0, 15)
    gather_steps(((2, 5),), ())
    multiply(1, 15, 25)
    gather_steps(((2, 6),), ())
    rs_first(1)
    contract(1)
    ar(1, 0)
    rs_second(0)
    ar(0, 2)
    ar(1, 1)
    from_sibling(2)
    multiply(2, 0, 25)
    rs_first(2)
    contract(2)
    ar(2, 0)
    ar(0, 3)
    ar(2, 1)
    rs_second(1)
    ar(1, 2)
    panel(0)
    rs_second(2)
    ar(2, 2)
    ar(1, 3)
    ar(0, 4)
    panel(1)
    ar(2, 3)
    ar(0, 5)
    diag_copy.wait()
    y00 = diag[0] - summed(f0, 2)
    y10 = -(summed(f0, 0).T + times(y00, new[1, 0]))
    super_out[0] = y00
    super_out[1] = y10
    y20 = -(summed(f0, 1).T + (times(y00, new[2, 0]) + times(y10, new[2, 1])))
    super_out[3] = y20
    super_out[2] = diag[1] - times(y10, new[1, 0], True)
    super_out[4] = times(y10.T, new[2, 0])
    super_out[5] = diag[2] - times(y20, new[2, 0], True)
    def send_done(t, n):
        pltpu.make_async_remote_copy(
            lo[t].at[0], lo[t].at[0], lo_send.at[t, n], lo_recv.at[t, 0],
            device_id=sib, device_id_type=MESH,
        ).wait_send()

    @pl.when(is_src & (k == src_k))
    def _():
        for t in range(3):
            for s in range(2):
                send_done(t, 30 + s)

    @pl.when(is_src)
    def _():
        for t, n in sent["src"]:
            send_done(t, n)

    @pl.when(jnp.logical_not(is_src))
    def _():
        for t, n in sent["mid"]:
            send_done(t, n)

    ar(1, 4)
    ar(2, 4)
    panel(2)
    ar(1, 5)
    y11 = super_out[2] - summed(f1, 1)
    super_out[2] = y11
    y21 = -(summed(f1, 0).T + (super_out[4] + times(y11, new[2, 1])))
    super_out[4] = y21
    rest = super_out[5] - times(y21, new[2, 1], True)
    for t in range(3):
        for n in range(6):
            rs_copy(t, n).wait_send()
    ar(2, 5)
    super_out[5] = rest - summed(f2, 0)


def place_kernel(found, out):
    for i in range(3):
        for j in range(3):
            out[i, j] = found[i * (i + 1) // 2 + j] if j <= i else jnp.zeros((256, 256), F32)


def per_device(
    inverse_blocks,
    inverse_rows,
    inverse_cols,
    inverse_count,
    panel_rows,
    lower_old,
    lower_new,
    diag_inverse,
):
    vmem = pl.BlockSpec(memory_space=pltpu.VMEM)
    hbm = pl.BlockSpec(memory_space=pltpu.HBM)

    def sent(*shape):
        return [
            pltpu.VMEM(tuple(nb if s is None else s for s in shape), kind) for nb, kind in zip(BUNDLES, KINDS)
        ]

    def each(*shape):
        return [pltpu.VMEM(tuple(nb if s is None else s for s in shape), F32) for nb in BUNDLES]

    panels, found = pl.pallas_call(
        kernel,
        out_shape=(
            jax.ShapeDtypeStruct((3, 2, 64, 256), BF16),
            jax.ShapeDtypeStruct((6, 256, 256), F32),
        ),
        in_specs=[hbm] * 8,
        out_specs=(vmem, vmem),
        scratch_shapes=[
            pltpu.VMEM((1, 96), jnp.int32),
            pltpu.VMEM((1, 96), jnp.int32),
            pltpu.SMEM((1, 1), jnp.int32),
            pltpu.SMEM((64,), jnp.int32),
            pltpu.VMEM((3, 2, 256, 256), BF16),
            pltpu.VMEM((3, 128), jnp.int32),
            pltpu.SMEM((3, 128), jnp.int32),
            pltpu.VMEM((97, 256, 256), BF16),
            *[pltpu.VMEM((16, 256, 256), BF16)] * 3,
            *[pltpu.VMEM((2, 256, 256), F32)] * 3,
            pltpu.VMEM((3, 3, 256, 256), BF16),
            pltpu.VMEM((3, 256, 256), F32),
            pltpu.VMEM((3, 64, 256), F32),
            pltpu.VMEM((3, 64, 256), F32),
            pltpu.VMEM((3, 2, 64, 256), F32),
            pltpu.VMEM((3, 2, 64, 256), F32),
            pltpu.VMEM((3, 128, 256), BF16),
            pltpu.VMEM((3, 256, 512), BF16),
            pltpu.VMEM((3, 512, 256), BF16),
            pltpu.VMEM((3, 512, 256), BF16),
            *each(None, 256, 256),
            *each(None, 128, 256),
            *sent(None, 16, 8, 256),
            *sent(16, None, 8, 256),
            *each(None, 8, 256),
            *each(4, None, 8, 256),
            *sent(None, 32, 8, 256),
            pltpu.SemaphoreType.DMA((9,)),
            pltpu.SemaphoreType.DMA((3, 32)),
            pltpu.SemaphoreType.DMA((3, 16)),
            pltpu.SemaphoreType.DMA((3, 6)),
            pltpu.SemaphoreType.DMA((3, 6)),
            pltpu.SemaphoreType.DMA((3, 7)),
            pltpu.SemaphoreType.DMA((3, 7)),
        ],
        compiler_params=pltpu.CompilerParams(
            collective_id=0, has_side_effects=True, vmem_limit_bytes=60 * 2**20
        ),
    )(inverse_rows, inverse_cols, inverse_count, panel_rows, lower_old, inverse_blocks, lower_new, diag_inverse)
    placed = pl.pallas_call(
        place_kernel,
        out_shape=jax.ShapeDtypeStruct((3, 3, 256, 256), F32),
        in_specs=[vmem],
        out_specs=vmem,
    )(found)
    return panels, placed


def solution(mesh):
    placed = (
        P("row", "col", None, None),
        P("row", "col"),
        P("row", "col"),
        P("row", "col"),
        P(),
        P(None, "row", None, None),
        P(),
        P(),
    )
    return jax.shard_map(
        per_device,
        mesh=mesh,
        in_specs=placed,
        out_specs=(P(None, "row", "col", None), P()),
        check_vma=False,
    )
```
